32 devices in a mesh: lat: 4 (over y, x), lon: 8 (over z, core).
Axes of the slice: x: 2, y: 2, z: 4, core: 2. Of those that a mesh axis runs over, the one named last changes fastest.
Arguments:
- fields: bfloat16 [16, 720, 641], P('lat', 'lon'), may hold values from -36 to 36
- group_size: int32 [8], replicated, may hold values from 1 to 121, 641 in all
- band_of_row: int32 [16], P('lat'), may hold values from 0 to 7, never falling along the last dimension, each value on 1 to 4 neighbouring positions
- basis_spectra: float32 [8, 9, 8, 2, 361], replicated, may hold values from -0.75 to 0.75
- basis_coef: float32 [641, 8], replicated, may hold values from -5 to 5
- mlp_gain: float32 [641], replicated, may hold values from 0.25 to 1.75
- w_in: bfloat16 [641, 1282], replicated, may hold values from -0.25 to 0.25
- w_out: bfloat16 [1282, 641], replicated, may hold values from -0.15625 to 0.15625
Outputs:
- block_out: bfloat16 [16, 720, 641], P('lat', 'lon')
The draws below stay inside these ranges and needn't reach their ends.
Inputs may be any that keep to these rules, and one draw needn't show every extreme that they name: `group_size`: group j holds the channels that follow those of groups 0 to j - 1; the sizes sum to 641. `band_of_row`: band numbers never fall along latitude; every band covers 1 to 4 rows.
All inputs are finite; a program needn't handle non-finite values.
Results may differ from the reference program's by a relative error of at most 0.0051.
Values may be sent and summed in bfloat16 or wider, within the bound.
A program may use at most 64 MiB of HBM per device.

```python
import math
import jax
import jax.numpy as jnp
import numpy as np
from jax import lax

C = 641
HIDDEN_UNITS = 1282
NLON = 720
HALO = 4
NBASIS = 8
BANDS = 8
NLAT = 16
GROUPS = 8
GMAX = 121
FREQ = 361
BAND_MOST = 4


def draw_fields(key, part):
    key_base = jax.random.fold_in(key, 11)
    key_chan = jax.random.fold_in(key, 12)
    key_lon = jax.random.fold_in(key, 13)
    chan_scale = jnp.exp(jax.random.uniform(key_chan, (C,), jnp.float32, math.log(0.3), math.log(3.0)))
    lon_scale = jnp.exp(jax.random.uniform(key_lon, (NLON, 1), jnp.float32, math.log(0.3), math.log(3.0)))
    base = jnp.clip(jax.random.normal(key_base, (NLAT, NLON, C), jnp.float32), -4.0, 4.0)
    return (base * lon_scale * chan_scale).astype(jnp.bfloat16)


def length_profile(amount, total, most, lean):
    weights = [(1 << 20) // math.isqrt(grade ** lean) + 1 for grade in range(2, amount + 1)]
    rest, given = total - most - (amount - 1), [1] * (amount - 1)
    while rest > 0:
        candidates = [i for i in range(amount - 1) if given[i] < most]
        mass, left = sum([weights[i] for i in candidates]), rest
        for i in candidates:
            more = min(most - given[i], max(1, left * weights[i] // mass), rest)
            given[i] = given[i] + more
            rest = rest - more
    return np.array([most] + given)


def uneven_parts(own_key, number_of, total, reach, slope):
    if number_of == 2:
        one = jax.random.randint(own_key, (), max(1, total - reach), min(reach, total - 1) + 1)
        return jnp.stack([one, total - one])
    lengths = jnp.asarray(length_profile(number_of, total, reach, slope), jnp.int32)
    twos = (number_of - 1) // 2
    giver, receiver = lengths[1:1 + 2 * twos:2], lengths[2:2 + 2 * twos:2]
    margin = jnp.minimum(giver - 1, reach - receiver)
    moved = jax.random.randint(jax.random.fold_in(own_key, 1), (twos,), 0, 1 << 20) % (margin + 1)
    lengths = lengths.at[1:1 + 2 * twos:2].set(giver - moved).at[2:2 + 2 * twos:2].set(receiver + moved)
    return lengths[jax.random.permutation(jax.random.fold_in(own_key, 2), number_of)]


def noise(rng, dims, scale, most, held_as=jnp.bfloat16):
    return jnp.clip(scale * jax.random.normal(rng, dims, jnp.float32), -most, most).astype(held_as)


def setup_inputs(seed: int = 0) -> dict:
    key_list = jax.random.split(jax.random.key(seed), 9)
    fields = draw_fields(jax.random.fold_in(key_list[8], 71), 0)
    group_size = uneven_parts(key_list[1], GROUPS, C, GMAX, 2).astype(jnp.int32)
    band_of_row = jnp.searchsorted(jnp.cumsum(uneven_parts(key_list[2], BANDS, NLAT, BAND_MOST, 1)), jnp.arange(NLAT), side="right").astype(jnp.int32)
    basis_spectra = noise(key_list[3], (BANDS, 2 * HALO + 1, NBASIS, 2, FREQ), ((2 * HALO + 1) * NBASIS) ** -0.5, 0.75, jnp.float32)
    basis_coef = noise(key_list[4], (C, NBASIS), 1.0, 5.0, jnp.float32)
    mlp_gain = jnp.clip(1.0 + 0.15 * jax.random.normal(key_list[5], (C,), jnp.float32), 0.25, 1.75)
    w_in = noise(key_list[6], (C, HIDDEN_UNITS), C ** -0.5, 0.25)
    w_out = noise(key_list[7], (HIDDEN_UNITS, C), HIDDEN_UNITS ** -0.5, 0.15625)
    return {"fields": fields, "group_size": group_size, "band_of_row": band_of_row, "basis_spectra": basis_spectra, "basis_coef": basis_coef, "mlp_gain": mlp_gain, "w_in": w_in, "w_out": w_out}


EPSILON = 1e-05

def reference(fields, group_size, band_of_row, basis_spectra, basis_coef, mlp_gain, w_in, w_out):
    values = fields.astype(jnp.float32)
    starts = (jnp.cumsum(group_size) - group_size).astype(jnp.int32)
    channel = jnp.arange(C, dtype=jnp.int32)
    group_of = (lax.optimization_barrier(jnp.sum((channel[:, None] >= starts[None, :]).astype(jnp.int32), axis=1)) - 1).astype(jnp.int32)
    member = (group_of[:, None] == jnp.arange(GROUPS, dtype=jnp.int32)[None, :]).astype(values.dtype)
    counts = group_size.astype(values.dtype) * NLON
    sums = lax.optimization_barrier(jnp.sum(values, axis=1))
    means = jnp.dot(sums, member, precision=lax.Precision.HIGHEST) / counts
    centred = values - jnp.take(means, group_of, axis=1)[:, None, :]
    squares = jnp.dot(lax.optimization_barrier(jnp.sum(centred * centred, axis=1)), member, precision=lax.Precision.HIGHEST) / counts
    scaled = jnp.take(lax.rsqrt(squares + EPSILON), group_of, axis=1)
    normed = centred * scaled[:, None, :]
    spectrum = jnp.fft.rfft(normed, axis=1)
    padding = ((HALO, HALO), (0, 0), (0, 0))
    pad_real = jnp.pad(jnp.real(spectrum), padding)
    pad_imag = jnp.pad(jnp.imag(spectrum), padding)
    taps = 2 * HALO + 1

    def one_row(row_index):
        basis = lax.dynamic_index_in_dim(basis_spectra, band_of_row[row_index], 0, keepdims=False)
        kernel = jnp.einsum('cb,dbpk->dpkc', basis_coef, basis, precision=lax.Precision.HIGHEST)
        win_real = lax.dynamic_slice_in_dim(pad_real, row_index, taps, 0)
        win_imag = lax.dynamic_slice_in_dim(pad_imag, row_index, taps, 0)
        out_real = lax.optimization_barrier(jnp.sum(kernel[:, 0] * win_real - kernel[:, 1] * win_imag, axis=0))
        out_imag = lax.optimization_barrier(jnp.sum(kernel[:, 0] * win_imag + kernel[:, 1] * win_real, axis=0))
        return (out_real, out_imag)
    prod_real, prod_imag = lax.map(one_row, jnp.arange(NLAT, dtype=jnp.int32))
    corr = jnp.fft.irfft(prod_real + 1j * prod_imag, n=NLON, axis=1).astype(values.dtype)
    mixed = (values + corr).astype(jnp.bfloat16)
    mixed = lax.optimization_barrier(mixed)

    def mlp_row(row_block):
        inputs = row_block.astype(jnp.float32)
        centre = lax.optimization_barrier(jnp.mean(inputs, axis=-1, keepdims=True))
        spread = lax.optimization_barrier(jnp.mean((inputs - centre) ** 2, axis=-1, keepdims=True))
        normalised = ((inputs - centre) * lax.rsqrt(spread + EPSILON) * mlp_gain).astype(jnp.bfloat16)
        hidden = jax.nn.gelu(jnp.dot(normalised, w_in, preferred_element_type=jnp.float32), approximate=False).astype(jnp.bfloat16)
        return (inputs + jnp.dot(hidden, w_out, preferred_element_type=jnp.float32)).astype(jnp.bfloat16)
    return lax.map(mlp_row, mixed)
```

```python
import functools
import math

import jax
import jax.numpy as jnp
import numpy as np
from jax import lax
from jax.experimental import pallas as pl
from jax.experimental.pallas import tpu as pltpu
from jax.sharding import PartitionSpec as P

HALO = 4
TAPS = 2 * HALO + 1
EPSILON = 1e-05
SUB = 8
VMEM = pl.BlockSpec(memory_space=pltpu.VMEM)
SMEM = pl.BlockSpec(memory_space=pltpu.SMEM)
ANY = pl.BlockSpec(memory_space=pl.ANY)
MESH = pl.DeviceIdType.MESH
DMA = pltpu.SemaphoreType.DMA


def round_up(value, step):
    return -(-value // step) * step


def dft_tables(lon_count, bins):
    freq = lon_count // 2 + 1
    phase = np.arange(lon_count)[:, None] * np.arange(freq)[None, :] % lon_count
    angle = phase * (2.0 * math.pi / lon_count)
    cosine = np.cos(angle)
    sine = np.where(2 * phase % lon_count == 0, 0.0, np.sin(angle))
    index = np.arange(freq)
    weight = np.where((index == 0) | (2 * index == lon_count), 1.0, 2.0) / lon_count
    table = np.zeros((lon_count, 2, bins), np.float64)
    table[:, 0, :freq] = cosine
    table[:, 1, :freq] = -sine
    table = table.reshape(lon_count, 2 * bins).astype(jnp.bfloat16)
    total = table.astype(np.float64).sum(axis=0, keepdims=True).astype(np.float32)
    scaled = np.zeros((2, bins), np.float32)
    scaled[:, :freq] = weight
    return table, total, scaled.reshape(1, 2 * bins)


def pixel_order(rows, cols):
    pixels = rows * cols
    index = np.arange(pixels)
    order = np.zeros((pixels, pixels), np.float32)
    order[index, index % rows * cols + index // rows] = 1.0
    return order.astype(jnp.bfloat16)


def place(index):
    pieces = lax.axis_size("lon")
    return (lax.div(index, pieces), lax.rem(index, pieces))


def own_index():
    return lax.axis_index("lat") * lax.axis_size("lon") + lax.axis_index("lon")


def drain(blocks, amount, semaphore):
    part = blocks.at[pl.ds(0, amount)]
    pltpu.make_async_copy(part, part, semaphore).wait()


def group_rows(size_ref, lanes, groups):
    group = lax.rem(lax.broadcasted_iota(jnp.int32, (1, lanes), 1), groups)
    start = jnp.zeros((1, lanes), jnp.int32)
    size = jnp.zeros((1, lanes), jnp.int32)
    for index in range(groups):
        start = start + jnp.where(group > index, size_ref[index], 0)
        size = size + jnp.where(group == index, size_ref[index], 0)
    return start, size


def membership(first, chan, start, size):
    channel = first + lax.broadcasted_iota(jnp.int32, (chan, start.shape[1]), 0)
    return (channel >= start) & (channel < start + size)


exact = functools.partial(
    lax.dot_general, precision=lax.Precision.HIGHEST, preferred_element_type=jnp.float32
)
OVER_FIRST = (((0,), (0,)), ((), ()))
OVER_LAST = (((1,), (1,)), ((), ()))


def block_body(
    devices, homes, chan, freq, bins, rows, cols, chan_count, groups,
    size_ref, band_ref,
    x_hbm, order_hbm, coef_hbm, basis_hbm, table_hbm, total_hbm, weight_hbm, gain_hbm,
    win_hbm, wout_hbm,
    out_ref,
    x_ref, order_ref, coef_ref, basis_ref, table_ref, total_ref, weight_ref, gain_ref,
    win_ref, wout_ref,
    flat_ref, arrived_ref, mixed_ref, returned_ref, report_ref, reports_ref,
    kern_ref, wide_ref, spec_ref, prod_ref, corr_ref,
    load_sem, block_send_sem, block_recv_sem, report_send_sem, report_recv_sem,
    mixed_send_sem, mixed_recv_sem, local_sem,
):
    me = own_index()
    pieces = lax.axis_size("lon")
    bands = devices // pieces
    lat = bands * rows
    parts = chan // SUB
    pixels = rows * cols
    band_count = basis_ref.shape[0] // TAPS
    own_home = lax.div(me * homes + devices - 1, devices)
    own_home = lax.rem(own_home, homes)
    is_home = lax.div(own_home * devices, homes) == me

    def device_of(home):
        return lax.div(home * devices, homes)

    loads = [
        pltpu.make_async_copy(source, target, load_sem.at[index])
        for index, (source, target) in enumerate(
            [
                (x_hbm, x_ref), (order_hbm, order_ref), (coef_hbm, coef_ref),
                (basis_hbm, basis_ref), (table_hbm, table_ref), (total_hbm, total_ref),
                (weight_hbm, weight_ref), (gain_hbm, gain_ref), (win_hbm, win_ref),
                (wout_hbm, wout_ref),
            ]
        )
    ]
    for load in loads:
        load.start()
    barrier = pltpu.get_barrier_semaphore()

    def greet(step, carry):
        pl.semaphore_signal(
            barrier, inc=1, device_id=place(lax.rem(me + step, devices)), device_id_type=MESH
        )
        return carry

    lax.fori_loop(1, devices, greet, 0)
    loads[0].wait()
    loads[1].wait()
    x = x_ref[...].reshape(pixels, chan_count)
    turned = lax.dot_general(
        x, order_ref[...], OVER_FIRST, preferred_element_type=jnp.float32
    ).astype(jnp.bfloat16)
    flat_ref[...] = jnp.zeros_like(flat_ref)
    flat_ref[:chan_count] = turned
    pl.semaphore_wait(barrier, devices - 1)

    def send_part(part):
        def send(step, carry):
            home = lax.rem(own_home + step, homes)
            target = device_of(home)

            @pl.when(target != me)
            def _():
                pltpu.make_async_remote_copy(
                    src_ref=flat_ref.at[pl.ds(pl.multiple_of(home * chan + part * SUB, SUB), SUB)],
                    dst_ref=arrived_ref.at[part, me],
                    send_sem=block_send_sem,
                    recv_sem=block_recv_sem.at[part],
                    device_id=place(target),
                    device_id_type=MESH,
                ).start()

            return carry

        lax.fori_loop(0, homes, send, 0)

    send_part(0)

    @pl.when(is_home)
    def _():
        for part in range(parts):
            first = pl.multiple_of(own_home * chan + part * SUB, SUB)
            pltpu.make_async_copy(
                flat_ref.at[pl.ds(first, SUB)], arrived_ref.at[part, me], local_sem.at[part]
            ).start()

    lane = lax.broadcasted_iota(jnp.int32, (pixels, 128), 0)
    slot = lax.broadcasted_iota(jnp.int32, (pixels, 128), 1)
    segment = (lane >= slot * cols) & (lane < (slot + 1) * cols)
    segment = jnp.where(segment, 1.0, 0.0).astype(jnp.bfloat16)

    def add_up(cells):
        return jnp.dot(cells, segment, preferred_element_type=jnp.float32)

    cells = flat_ref[...]
    means = add_up(cells) / cols
    near = means.astype(jnp.bfloat16)
    spread_out = lax.dot_general(near, segment, OVER_LAST, preferred_element_type=jnp.float32)
    offset = cells.astype(jnp.float32) - spread_out
    square = offset * offset
    high = square.astype(jnp.bfloat16)
    low = (square - high.astype(jnp.float32)).astype(jnp.bfloat16)
    shift = means - near.astype(jnp.float32)
    squares = jnp.maximum(add_up(high) + add_up(low) - cols * shift * shift, 0.0)
    start, size = group_rows(size_ref, 128, groups)
    member = jnp.where(
        membership(0, homes * chan, start, size)
        & (lax.broadcasted_iota(jnp.int32, (1, 128), 1) < groups),
        1.0, 0.0,
    )
    centre = exact(means, member, OVER_FIRST) / jnp.maximum(size, 1).astype(jnp.float32)
    offset = means - exact(member, centre, OVER_LAST)
    spread = exact(squares + cols * offset * offset, member, OVER_FIRST)
    lanes = report_ref.shape[1]
    rest = lanes - 2 * rows * groups
    place_of = lax.broadcasted_iota(jnp.int32, (1, rest), 1)
    numbers = jnp.zeros((1, rest), jnp.float32)
    for row in range(rows):
        numbers = jnp.where(place_of == row, band_ref[row].astype(jnp.float32), numbers)
    report = jnp.concatenate(
        [centre[row : row + 1, :groups] for row in range(rows)]
        + [spread[row : row + 1, :groups] for row in range(rows)]
        + [numbers],
        axis=1,
    )
    report_ref[...] = report
    reports_ref[me] = report

    for part in range(1, parts):
        send_part(part)

    def tell(step, carry):
        pltpu.make_async_remote_copy(
            src_ref=report_ref,
            dst_ref=reports_ref.at[me],
            send_sem=report_send_sem,
            recv_sem=report_recv_sem,
            device_id=place(lax.rem(me + step, devices)),
            device_id_type=MESH,
        ).start()
        return carry

    lax.fori_loop(1, devices, tell, 0)

    loads[2].wait()
    loads[3].wait()
    wanted = own_home * chan + lax.broadcasted_iota(jnp.int32, (chan, chan_count), 0)
    chosen = jnp.where(
        lax.broadcasted_iota(jnp.int32, (chan, chan_count), 1) == wanted, 1.0, 0.0
    )
    coef = exact(chosen, coef_ref[...], OVER_LAST)
    high = coef.astype(jnp.bfloat16).astype(jnp.float32)
    coef = jnp.concatenate([high, coef - high, high], axis=1).astype(jnp.bfloat16)
    blank = jnp.zeros((basis_ref.shape[1], bins - freq), jnp.float32)

    def generate(n, carry):
        basis = jnp.concatenate(
            [basis_ref[n, :, 0, :], blank, basis_ref[n, :, 1, :], blank], axis=1
        )
        high = basis.astype(jnp.bfloat16).astype(jnp.float32)
        both = jnp.concatenate([high, high, basis - high], axis=0).astype(jnp.bfloat16)
        made = jnp.dot(coef, both, preferred_element_type=jnp.float32)
        kern_ref[n, :chan] = made[:, :bins]
        kern_ref[n, chan:] = made[:, bins:]
        return carry

    lax.fori_loop(0, basis_ref.shape[0], generate, 0, unroll=3)
    for load in loads[4:]:
        load.wait()
    drain(reports_ref, devices - 1, report_send_sem)
    drain(reports_ref, devices - 1, report_recv_sem)

    @pl.when(is_home)
    def _():
        start, size = group_rows(size_ref, lanes, groups)
        amount = size.astype(jnp.float32) * cols
        lane = lax.broadcasted_iota(jnp.int32, (1, lanes), 1)
        seen = []
        for band in range(bands):
            report = reports_ref[band * pieces : (band + 1) * pieces, 0]
            centre = jnp.sum(report, axis=0, keepdims=True) / pieces
            offset = report - centre
            between = amount * jnp.sum(offset * offset, axis=0, keepdims=True)
            within = jnp.sum(report, axis=0, keepdims=True)
            seen.append((report, centre, between, within))
        band_of = []
        for band in range(bands):
            for row in range(rows):
                mark = lane == 2 * rows * groups + row
                number = jnp.sum(jnp.where(mark, seen[band][0][:1], 0.0)).astype(jnp.int32)
                band_of.append(jnp.clip(number, 0, band_count - 1))
        for part in range(parts):
            pltpu.make_async_copy(
                flat_ref.at[pl.ds(0, SUB)], arrived_ref.at[part, me], local_sem.at[part]
            ).wait()
            drain(arrived_ref.at[part], devices - 1, block_recv_sem.at[part])
            member = membership(own_home * chan + part * SUB, SUB, start, size)
            for band in range(bands):
                for piece in range(pieces):
                    cells = arrived_ref[part, band * pieces + piece].astype(jnp.float32)
                    for row in range(rows):
                        at = (band * rows + row) * SUB
                        wide_ref[at : at + SUB, piece * cols : (piece + 1) * cols] = cells[
                            :, row * cols : (row + 1) * cols
                        ]
            raw = jnp.dot(
                wide_ref[...].astype(jnp.bfloat16), table_ref[...],
                preferred_element_type=jnp.float32,
            )
            for band in range(bands):
                _, centre, between, within = seen[band]
                for row in range(rows):
                    low, high = row * groups, (rows + row) * groups
                    here = member & (lane >= low) & (lane < low + groups)
                    there = member & (lane >= high) & (lane < high + groups)

                    def pick(mask, cells):
                        return jnp.sum(jnp.where(mask, cells, 0.0), axis=1, keepdims=True)

                    square = pick(here, between) + pick(there, within)
                    count = pick(here, amount) * pieces
                    mean = pick(here, centre)
                    scale = lax.rsqrt(square / jnp.maximum(count, 1.0) + EPSILON)
                    at = (band * rows + row) * SUB
                    spec_ref[at : at + SUB] = (raw[at : at + SUB] - mean * total_ref[...]) * scale
            for row in range(lat):
                real = jnp.zeros((SUB, bins), jnp.float32)
                imag = jnp.zeros((SUB, bins), jnp.float32)
                for tap in range(TAPS):
                    source = row + tap - HALO
                    if source < 0 or source >= lat:
                        continue
                    at = source * SUB
                    spec_real = spec_ref[at : at + SUB, :bins]
                    spec_imag = spec_ref[at : at + SUB, bins:]
                    index = band_of[row] * TAPS + tap
                    at = part * SUB
                    kern_real = kern_ref[index, at : at + SUB]
                    kern_imag = kern_ref[index, chan + at : chan + at + SUB]
                    real = real + kern_real * spec_real - kern_imag * spec_imag
                    imag = imag + kern_real * spec_imag + kern_imag * spec_real
                prod_ref[row * SUB : (row + 1) * SUB, :bins] = real
                prod_ref[row * SUB : (row + 1) * SUB, bins:] = imag
            corr_ref[...] = lax.dot_general(
                (prod_ref[...] * weight_ref[...]).astype(jnp.bfloat16),
                table_ref[...],
                OVER_LAST,
                preferred_element_type=jnp.float32,
            )
            for band in range(bands):
                for piece in range(pieces):
                    pieces_of = []
                    for row in range(rows):
                        at = (band * rows + row) * SUB
                        pieces_of.append(
                            corr_ref[at : at + SUB, piece * cols : (piece + 1) * cols]
                        )
                    device = band * pieces + piece
                    cells = arrived_ref[part, device].astype(jnp.float32)
                    mixed_ref[part, device] = (
                        cells + jnp.concatenate(pieces_of, axis=1)
                    ).astype(jnp.bfloat16)
            first = pl.multiple_of(own_home * chan + part * SUB, SUB)

            def give(step, carry):
                target = lax.rem(me + step, devices)
                pltpu.make_async_remote_copy(
                    src_ref=mixed_ref.at[part, target],
                    dst_ref=returned_ref.at[pl.ds(first, SUB)],
                    send_sem=mixed_send_sem,
                    recv_sem=mixed_recv_sem,
                    device_id=place(target),
                    device_id_type=MESH,
                ).start()
                return carry

            lax.fori_loop(1, devices, give, 0)
            pltpu.make_async_copy(
                mixed_ref.at[part, me], returned_ref.at[pl.ds(first, SUB)], local_sem.at[part]
            ).start()
        for part in range(parts):
            pltpu.make_async_copy(
                mixed_ref.at[part, me], returned_ref.at[pl.ds(0, SUB)], local_sem.at[part]
            ).wait()
            drain(mixed_ref.at[part], devices - 1, mixed_send_sem)
        drain(flat_ref, (homes - 1) * chan, block_send_sem)
        drain(returned_ref, (homes - 1) * chan, mixed_recv_sem)

    @pl.when(jnp.logical_not(is_home))
    def _():
        drain(flat_ref, homes * chan, block_send_sem)
        drain(returned_ref, homes * chan, mixed_recv_sem)

    step = pixels // 3 if pixels % 24 == 0 else pixels
    for at in range(0, pixels, step):
        inputs = lax.dot_general(
            order_ref[at : at + step, :], returned_ref[...], OVER_LAST,
            preferred_element_type=jnp.float32,
        )[:, :chan_count]
        centre = jnp.mean(inputs, axis=-1, keepdims=True)
        spread = jnp.mean((inputs - centre) ** 2, axis=-1, keepdims=True)
        normalised = (
            (inputs - centre) * lax.rsqrt(spread + EPSILON) * gain_ref[...]
        ).astype(jnp.bfloat16)
        hidden = jnp.dot(normalised, win_ref[...], preferred_element_type=jnp.float32)
        hidden = (0.5 * hidden * (1.0 + lax.erf(hidden * math.sqrt(0.5)))).astype(jnp.bfloat16)
        result = inputs + lax.dot_general(
            hidden, wout_ref[...], OVER_LAST, preferred_element_type=jnp.float32
        )
        out_ref[at : at + step] = result.astype(jnp.bfloat16)


def per_device(fields, group_size, band_of_row, basis_spectra, basis_coef, mlp_gain, w_in, w_out):
    row_count, col_count, chan_count = fields.shape
    pieces = lax.axis_size("lon")
    bands = lax.axis_size("lat")
    devices = pieces * bands
    lon_count = col_count * pieces
    lat_count = row_count * bands
    freq_count = lon_count // 2 + 1
    groups = group_size.shape[0]
    pixels = row_count * col_count
    chan = round_up(-(-chan_count // devices), SUB)
    homes = -(-chan_count // chan)
    parts = chan // SUB
    bins = round_up(freq_count, 128)
    band_count, _, basis_count = basis_spectra.shape[:3]
    hidden = w_in.shape[1]
    lanes = round_up((2 * groups + 1) * row_count, 128)
    table, total, weight = dft_tables(lon_count, bins)
    basis = basis_spectra.reshape(band_count * TAPS, basis_count, 2, freq_count)
    f32, bf16 = jnp.float32, jnp.bfloat16
    operands = [
        (jnp.transpose(fields, (1, 0, 2)), bf16),
        (pixel_order(row_count, col_count), bf16),
        (basis_coef.T, f32),
        (basis, f32),
        (table, bf16),
        (total, f32),
        (weight, f32),
        (mlp_gain.reshape(1, chan_count), f32),
        (w_in, bf16),
        (w_out.T, bf16),
    ]
    out = pl.pallas_call(
        functools.partial(
            block_body, devices, homes, chan, freq_count, bins, row_count, col_count,
            chan_count, groups,
        ),
        out_shape=jax.ShapeDtypeStruct((pixels, chan_count), bf16),
        in_specs=[SMEM] * 2 + [ANY] * len(operands),
        out_specs=VMEM,
        scratch_shapes=[pltpu.VMEM(array.shape, kind) for array, kind in operands]
        + [
            pltpu.VMEM((homes * chan, pixels), bf16),
            pltpu.VMEM((parts, devices, SUB, pixels), bf16),
            pltpu.VMEM((parts, devices, SUB, pixels), bf16),
            pltpu.VMEM((homes * chan, pixels), bf16),
            pltpu.VMEM((1, lanes), f32),
            pltpu.VMEM((devices, 1, lanes), f32),
            pltpu.VMEM((band_count * TAPS, 2 * chan, bins), f32),
            pltpu.VMEM((lat_count * SUB, lon_count), f32),
            pltpu.VMEM((lat_count * SUB, 2 * bins), f32),
            pltpu.VMEM((lat_count * SUB, 2 * bins), f32),
            pltpu.VMEM((lat_count * SUB, lon_count), f32),
            DMA((len(operands),)),
            DMA,
            DMA((parts,)),
            DMA,
            DMA,
            DMA,
            DMA,
            DMA((parts,)),
        ],
        compiler_params=pltpu.CompilerParams(
            collective_id=0, has_side_effects=True, vmem_limit_bytes=60 * 1024 * 1024
        ),
    )(group_size, band_of_row, *[array for array, _ in operands])
    return jnp.transpose(out.reshape(col_count, row_count, chan_count), (1, 0, 2))


def solution(mesh):
    placed = (P("lat", "lon", None), P(), P("lat"), P(), P(), P(), P(), P())
    return jax.shard_map(
        per_device, mesh=mesh, in_specs=placed, out_specs=P("lat", "lon", None), check_vma=False
    )
```

```python
import functools
import math

import jax
import jax.numpy as jnp
import numpy as np
from jax import lax
from jax.experimental import pallas as pl
from jax.experimental.pallas import tpu as pltpu
from jax.sharding import PartitionSpec as P

HALO = 4
TAPS = 2 * HALO + 1
EPSILON = 1e-05
SUB = 8
VMEM = pl.BlockSpec(memory_space=pltpu.VMEM)
SMEM = pl.BlockSpec(memory_space=pltpu.SMEM)
HBM = pl.BlockSpec(memory_space=pltpu.HBM)
MESH = pl.DeviceIdType.MESH
DMA = pltpu.SemaphoreType.DMA


def round_up(value, step):
    return -(-value // step) * step


def dft_tables(lon_count, bins):
    freq = lon_count // 2 + 1
    phase = np.arange(lon_count)[:, None] * np.arange(freq)[None, :] % lon_count
    angle = phase * (2.0 * math.pi / lon_count)
    cosine = np.cos(angle)
    sine = np.where(2 * phase % lon_count == 0, 0.0, np.sin(angle))
    index = np.arange(freq)
    weight = np.where((index == 0) | (2 * index == lon_count), 1.0, 2.0) / lon_count
    table = np.zeros((lon_count, 2, bins), np.float64)
    table[:, 0, :freq] = cosine
    table[:, 1, :freq] = -sine
    table = table.reshape(lon_count, 2 * bins).astype(jnp.bfloat16)
    total = table.astype(np.float64).sum(axis=0, keepdims=True).astype(np.float32)
    scaled = np.zeros((2, bins), np.float32)
    scaled[:, :freq] = weight
    return table, total, scaled.reshape(1, 2 * bins)


def pixel_order(rows, cols):
    pixels = rows * cols
    index = np.arange(pixels)
    order = np.zeros((pixels, pixels), np.float32)
    order[index, index % rows * cols + index // rows] = 1.0
    return order.astype(jnp.bfloat16)


def place(index):
    pieces = lax.axis_size("lon")
    return (lax.div(index, pieces), lax.rem(index, pieces))


def own_index():
    return lax.axis_index("lat") * lax.axis_size("lon") + lax.axis_index("lon")


def drain(blocks, amount, semaphore):
    part = blocks.at[pl.ds(0, amount)]
    pltpu.make_async_copy(part, part, semaphore).wait()


def group_rows(size_ref, lanes, groups):
    group = lax.rem(lax.broadcasted_iota(jnp.int32, (1, lanes), 1), groups)
    start = jnp.zeros((1, lanes), jnp.int32)
    size = jnp.zeros((1, lanes), jnp.int32)
    for index in range(groups):
        start = start + jnp.where(group > index, size_ref[index], 0)
        size = size + jnp.where(group == index, size_ref[index], 0)
    return start, size


def membership(first, chan, start, size):
    channel = first + lax.broadcasted_iota(jnp.int32, (chan, start.shape[1]), 0)
    return (channel >= start) & (channel < start + size)


exact = functools.partial(
    lax.dot_general, precision=lax.Precision.HIGHEST, preferred_element_type=jnp.float32
)
OVER_FIRST = (((0,), (0,)), ((), ()))
OVER_LAST = (((1,), (1,)), ((), ()))


def block_body(
    devices, homes, chan, freq, bins, rows, cols, chan_count, groups,
    size_ref, band_ref,
    x_hbm, order_hbm, coef_hbm, basis_hbm, table_hbm, total_hbm, weight_hbm, gain_hbm,
    win_hbm, wout_hbm,
    out_ref,
    x_ref, order_ref, coef_ref, basis_ref, table_ref, total_ref, weight_ref, gain_ref,
    win_ref, wout_ref,
    flat_ref, arrived_ref, mixed_ref, returned_ref, report_ref, reports_ref,
    kern_ref, wide_ref, spec_ref, prod_ref, corr_ref,
    load_sem, block_send_sem, block_recv_sem, report_send_sem, report_recv_sem,
    mixed_send_sem, mixed_recv_sem, local_sem,
):
    me = own_index()
    pieces = lax.axis_size("lon")
    bands = devices // pieces
    lat = bands * rows
    parts = chan // SUB
    pixels = rows * cols
    band_count = basis_ref.shape[0] // TAPS
    own_home = lax.div(me * homes + devices - 1, devices)
    own_home = lax.rem(own_home, homes)
    is_home = lax.div(own_home * devices, homes) == me

    def device_of(home):
        return lax.div(home * devices, homes)

    loads = [
        pltpu.make_async_copy(source, target, load_sem.at[index])
        for index, (source, target) in enumerate(
            [
                (x_hbm, x_ref), (order_hbm, order_ref), (coef_hbm, coef_ref),
                (basis_hbm, basis_ref), (table_hbm, table_ref), (total_hbm, total_ref),
                (weight_hbm, weight_ref), (gain_hbm, gain_ref), (win_hbm, win_ref),
                (wout_hbm, wout_ref),
            ]
        )
    ]
    for load in loads:
        load.start()
    barrier = pltpu.get_barrier_semaphore()

    def greet(step, carry):
        pl.semaphore_signal(
            barrier, inc=1, device_id=place(lax.rem(me + step, devices)), device_id_type=MESH
        )
        return carry

    lax.fori_loop(1, devices, greet, 0)
    loads[0].wait()
    loads[1].wait()
    x = x_ref[...].reshape(pixels, chan_count)
    turned = lax.dot_general(
        x, order_ref[...], OVER_FIRST, preferred_element_type=jnp.float32
    ).astype(jnp.bfloat16)
    flat_ref[...] = jnp.zeros_like(flat_ref)
    flat_ref[:chan_count] = turned
    pl.semaphore_wait(barrier, devices - 1)

    def send_part(part):
        def send(step, carry):
            home = lax.rem(own_home + step, homes)
            target = device_of(home)

            @pl.when(target != me)
            def _():
                pltpu.make_async_remote_copy(
                    src_ref=flat_ref.at[pl.ds(pl.multiple_of(home * chan + part * SUB, SUB), SUB)],
                    dst_ref=arrived_ref.at[part, me],
                    send_sem=block_send_sem,
                    recv_sem=block_recv_sem.at[part],
                    device_id=place(target),
                    device_id_type=MESH,
                ).start()

            return carry

        lax.fori_loop(0, homes, send, 0)

    send_part(0)

    @pl.when(is_home)
    def _():
        for part in range(parts):
            first = pl.multiple_of(own_home * chan + part * SUB, SUB)
            pltpu.make_async_copy(
                flat_ref.at[pl.ds(first, SUB)], arrived_ref.at[part, me], local_sem.at[part]
            ).start()

    lane = lax.broadcasted_iota(jnp.int32, (pixels, 128), 0)
    slot = lax.broadcasted_iota(jnp.int32, (pixels, 128), 1)
    segment = (lane >= slot * cols) & (lane < (slot + 1) * cols)
    segment = jnp.where(segment, 1.0, 0.0).astype(jnp.bfloat16)

    def add_up(cells):
        return jnp.dot(cells, segment, preferred_element_type=jnp.float32)

    cells = flat_ref[...]
    means = add_up(cells) / cols
    near = means.astype(jnp.bfloat16)
    spread_out = lax.dot_general(near, segment, OVER_LAST, preferred_element_type=jnp.float32)
    offset = cells.astype(jnp.float32) - spread_out
    square = offset * offset
    high = square.astype(jnp.bfloat16)
    low = (square - high.astype(jnp.float32)).astype(jnp.bfloat16)
    shift = means - near.astype(jnp.float32)
    squares = jnp.maximum(add_up(high) + add_up(low) - cols * shift * shift, 0.0)
    start, size = group_rows(size_ref, 128, groups)
    member = jnp.where(
        membership(0, homes * chan, start, size)
        & (lax.broadcasted_iota(jnp.int32, (1, 128), 1) < groups),
        1.0, 0.0,
    )
    centre = exact(means, member, OVER_FIRST) / jnp.maximum(size, 1).astype(jnp.float32)
    offset = means - exact(member, centre, OVER_LAST)
    spread = exact(squares + cols * offset * offset, member, OVER_FIRST)
    lanes = report_ref.shape[1]
    rest = lanes - 2 * rows * groups
    place_of = lax.broadcasted_iota(jnp.int32, (1, rest), 1)
    numbers = jnp.zeros((1, rest), jnp.float32)
    for row in range(rows):
        numbers = jnp.where(place_of == row, band_ref[row].astype(jnp.float32), numbers)
    report = jnp.concatenate(
        [centre[row : row + 1, :groups] for row in range(rows)]
        + [spread[row : row + 1, :groups] for row in range(rows)]
        + [numbers],
        axis=1,
    )
    report_ref[...] = report
    reports_ref[me] = report

    def tell(step, carry):
        pltpu.make_async_remote_copy(
            src_ref=report_ref,
            dst_ref=reports_ref.at[me],
            send_sem=report_send_sem,
            recv_sem=report_recv_sem,
            device_id=place(lax.rem(me + step, devices)),
            device_id_type=MESH,
        ).start()
        return carry

    lax.fori_loop(1, devices, tell, 0)
    for part in range(1, parts):
        send_part(part)

    loads[2].wait()
    loads[3].wait()
    wanted = own_home * chan + lax.broadcasted_iota(jnp.int32, (chan, chan_count), 0)
    chosen = jnp.where(
        lax.broadcasted_iota(jnp.int32, (chan, chan_count), 1) == wanted, 1.0, 0.0
    )
    coef = exact(chosen, coef_ref[...], OVER_LAST)
    high = coef.astype(jnp.bfloat16).astype(jnp.float32)
    coef = jnp.concatenate([high, coef - high, high], axis=1).astype(jnp.bfloat16)
    blank = jnp.zeros((basis_ref.shape[1], bins - freq), jnp.float32)

    def generate(n, carry):
        basis = jnp.concatenate(
            [basis_ref[n, :, 0, :], blank, basis_ref[n, :, 1, :], blank], axis=1
        )
        high = basis.astype(jnp.bfloat16).astype(jnp.float32)
        both = jnp.concatenate([high, high, basis - high], axis=0).astype(jnp.bfloat16)
        made = jnp.dot(coef, both, preferred_element_type=jnp.float32)
        kern_ref[n, :chan] = made[:, :bins]
        kern_ref[n, chan:] = made[:, bins:]
        return carry

    lax.fori_loop(0, basis_ref.shape[0], generate, 0, unroll=3)
    for load in loads[4:]:
        load.wait()
    drain(reports_ref, devices - 1, report_send_sem)
    drain(reports_ref, devices - 1, report_recv_sem)

    @pl.when(is_home)
    def _():
        start, size = group_rows(size_ref, lanes, groups)
        amount = size.astype(jnp.float32) * cols
        lane = lax.broadcasted_iota(jnp.int32, (1, lanes), 1)
        seen = []
        for band in range(bands):
            report = reports_ref[band * pieces : (band + 1) * pieces, 0]
            centre = jnp.sum(report, axis=0, keepdims=True) / pieces
            offset = report - centre
            between = amount * jnp.sum(offset * offset, axis=0, keepdims=True)
            within = jnp.sum(report, axis=0, keepdims=True)
            seen.append((report, centre, between, within))
        band_of = []
        for band in range(bands):
            for row in range(rows):
                mark = lane == 2 * rows * groups + row
                number = jnp.sum(jnp.where(mark, seen[band][0][:1], 0.0)).astype(jnp.int32)
                band_of.append(jnp.clip(number, 0, band_count - 1))
        for part in range(parts):
            pltpu.make_async_copy(
                flat_ref.at[pl.ds(0, SUB)], arrived_ref.at[part, me], local_sem.at[part]
            ).wait()
            drain(arrived_ref.at[part], devices - 1, block_recv_sem.at[part])
            member = membership(own_home * chan + part * SUB, SUB, start, size)
            for band in range(bands):
                for piece in range(pieces):
                    cells = arrived_ref[part, band * pieces + piece].astype(jnp.float32)
                    for row in range(rows):
                        at = (band * rows + row) * SUB
                        wide_ref[at : at + SUB, piece * cols : (piece + 1) * cols] = cells[
                            :, row * cols : (row + 1) * cols
                        ]
            raw = jnp.dot(
                wide_ref[...].astype(jnp.bfloat16), table_ref[...],
                preferred_element_type=jnp.float32,
            )
            for band in range(bands):
                _, centre, between, within = seen[band]
                for row in range(rows):
                    low, high = row * groups, (rows + row) * groups
                    here = member & (lane >= low) & (lane < low + groups)
                    there = member & (lane >= high) & (lane < high + groups)

                    def pick(mask, cells):
                        return jnp.sum(jnp.where(mask, cells, 0.0), axis=1, keepdims=True)

                    square = pick(here, between) + pick(there, within)
                    count = pick(here, amount) * pieces
                    mean = pick(here, centre)
                    scale = lax.rsqrt(square / jnp.maximum(count, 1.0) + EPSILON)
                    at = (band * rows + row) * SUB
                    spec_ref[at : at + SUB] = (raw[at : at + SUB] - mean * total_ref[...]) * scale
            for row in range(lat):
                real = jnp.zeros((SUB, bins), jnp.float32)
                imag = jnp.zeros((SUB, bins), jnp.float32)
                for tap in range(TAPS):
                    source = row + tap - HALO
                    if source < 0 or source >= lat:
                        continue
                    at = source * SUB
                    spec_real = spec_ref[at : at + SUB, :bins]
                    spec_imag = spec_ref[at : at + SUB, bins:]
                    index = band_of[row] * TAPS + tap
                    at = part * SUB
                    kern_real = kern_ref[index, at : at + SUB]
                    kern_imag = kern_ref[index, chan + at : chan + at + SUB]
                    real = real + kern_real * spec_real - kern_imag * spec_imag
                    imag = imag + kern_real * spec_imag + kern_imag * spec_real
                prod_ref[row * SUB : (row + 1) * SUB, :bins] = real
                prod_ref[row * SUB : (row + 1) * SUB, bins:] = imag
            corr_ref[...] = lax.dot_general(
                (prod_ref[...] * weight_ref[...]).astype(jnp.bfloat16),
                table_ref[...],
                OVER_LAST,
                preferred_element_type=jnp.float32,
            )
            for band in range(bands):
                for piece in range(pieces):
                    pieces_of = []
                    for row in range(rows):
                        at = (band * rows + row) * SUB
                        pieces_of.append(
                            corr_ref[at : at + SUB, piece * cols : (piece + 1) * cols]
                        )
                    device = band * pieces + piece
                    cells = arrived_ref[part, device].astype(jnp.float32)
                    mixed_ref[part, device] = (
                        cells + jnp.concatenate(pieces_of, axis=1)
                    ).astype(jnp.bfloat16)
            first = pl.multiple_of(own_home * chan + part * SUB, SUB)

            def give(step, carry):
                target = lax.rem(me + step, devices)
                pltpu.make_async_remote_copy(
                    src_ref=mixed_ref.at[part, target],
                    dst_ref=returned_ref.at[pl.ds(first, SUB)],
                    send_sem=mixed_send_sem,
                    recv_sem=mixed_recv_sem,
                    device_id=place(target),
                    device_id_type=MESH,
                ).start()
                return carry

            lax.fori_loop(1, devices, give, 0)
            pltpu.make_async_copy(
                mixed_ref.at[part, me], returned_ref.at[pl.ds(first, SUB)], local_sem.at[part]
            ).start()
        for part in range(parts):
            pltpu.make_async_copy(
                mixed_ref.at[part, me], returned_ref.at[pl.ds(0, SUB)], local_sem.at[part]
            ).wait()
            drain(mixed_ref.at[part], devices - 1, mixed_send_sem)
        drain(flat_ref, (homes - 1) * chan, block_send_sem)
        drain(returned_ref, (homes - 1) * chan, mixed_recv_sem)

    @pl.when(jnp.logical_not(is_home))
    def _():
        drain(flat_ref, homes * chan, block_send_sem)
        drain(returned_ref, homes * chan, mixed_recv_sem)

    step = pixels
    for at in range(0, pixels, step):
        inputs = lax.dot_general(
            order_ref[at : at + step, :], returned_ref[...], OVER_LAST,
            preferred_element_type=jnp.float32,
        )[:, :chan_count]
        centre = jnp.mean(inputs, axis=-1, keepdims=True)
        spread = jnp.mean((inputs - centre) ** 2, axis=-1, keepdims=True)
        normalised = (
            (inputs - centre) * lax.rsqrt(spread + EPSILON) * gain_ref[...].reshape(1, chan_count)
        ).astype(jnp.bfloat16)
        hidden = jnp.dot(normalised, win_ref[...], preferred_element_type=jnp.float32)
        hidden = (0.5 * hidden * (1.0 + lax.erf(hidden * math.sqrt(0.5)))).astype(jnp.bfloat16)
        result = inputs + lax.dot_general(
            hidden, wout_ref[...], OVER_LAST, preferred_element_type=jnp.float32
        )
        out_ref[at // rows : (at + step) // rows] = result.astype(jnp.bfloat16).reshape(
            step // rows, rows, chan_count
        )


def per_device(fields, group_size, band_of_row, basis_spectra, basis_coef, mlp_gain, w_in, w_out):
    row_count, col_count, chan_count = fields.shape
    pieces = lax.axis_size("lon")
    bands = lax.axis_size("lat")
    devices = pieces * bands
    lon_count = col_count * pieces
    lat_count = row_count * bands
    freq_count = lon_count // 2 + 1
    groups = group_size.shape[0]
    pixels = row_count * col_count
    chan = round_up(-(-chan_count // devices), SUB)
    homes = -(-chan_count // chan)
    parts = chan // SUB
    bins = round_up(freq_count, 128)
    band_count, _, basis_count = basis_spectra.shape[:3]
    hidden = w_in.shape[1]
    lanes = round_up((2 * groups + 1) * row_count, 128)
    table, total, weight = dft_tables(lon_count, bins)
    basis = basis_spectra.reshape(band_count * TAPS, basis_count, 2, freq_count)
    f32, bf16 = jnp.float32, jnp.bfloat16
    operands = [
        (jnp.transpose(fields, (1, 0, 2)), bf16),
        (pixel_order(row_count, col_count), bf16),
        (basis_coef.T, f32),
        (basis, f32),
        (table, bf16),
        (total, f32),
        (weight, f32),
        (mlp_gain, f32),
        (w_in, bf16),
        (w_out.T, bf16),
    ]
    out = pl.pallas_call(
        functools.partial(
            block_body, devices, homes, chan, freq_count, bins, row_count, col_count,
            chan_count, groups,
        ),
        out_shape=jax.ShapeDtypeStruct((col_count, row_count, chan_count), bf16),
        in_specs=[SMEM] * 2 + [HBM] * len(operands),
        out_specs=VMEM,
        scratch_shapes=[pltpu.VMEM(array.shape, kind) for array, kind in operands]
        + [
            pltpu.VMEM((homes * chan, pixels), bf16),
            pltpu.VMEM((parts, devices, SUB, pixels), bf16),
            pltpu.VMEM((parts, devices, SUB, pixels), bf16),
            pltpu.VMEM((homes * chan, pixels), bf16),
            pltpu.VMEM((1, lanes), f32),
            pltpu.VMEM((devices, 1, lanes), f32),
            pltpu.VMEM((band_count * TAPS, 2 * chan, bins), f32),
            pltpu.VMEM((lat_count * SUB, lon_count), f32),
            pltpu.VMEM((lat_count * SUB, 2 * bins), f32),
            pltpu.VMEM((lat_count * SUB, 2 * bins), f32),
            pltpu.VMEM((lat_count * SUB, lon_count), f32),
            DMA((len(operands),)),
            DMA,
            DMA((parts,)),
            DMA,
            DMA,
            DMA,
            DMA,
            DMA((parts,)),
        ],
        compiler_params=pltpu.CompilerParams(
            collective_id=0, has_side_effects=True, vmem_limit_bytes=60 * 1024 * 1024
        ),
    )(group_size, band_of_row, *[array for array, _ in operands])
    return jnp.transpose(out, (1, 0, 2))


def solution(mesh):
    placed = (P("lat", "lon", None), P(), P("lat"), P(), P(), P(), P(), P())
    return jax.shard_map(
        per_device, mesh=mesh, in_specs=placed, out_specs=P("lat", "lon", None), check_vma=False
    )
```

```python
import functools
import math

import jax
import jax.numpy as jnp
import numpy as np
from jax import lax
from jax.experimental import pallas as pl
from jax.experimental.pallas import tpu as pltpu
from jax.sharding import PartitionSpec as P

HALO = 4
TAPS = 2 * HALO + 1
EPSILON = 1e-05
SUB = 8
VMEM = pl.BlockSpec(memory_space=pltpu.VMEM)
HBM = pl.BlockSpec(memory_space=pltpu.HBM)
MESH = pl.DeviceIdType.MESH
DMA = pltpu.SemaphoreType.DMA


def round_up(value, step):
    return -(-value // step) * step


def dft_tables(lon_count, bins):
    freq = lon_count // 2 + 1
    phase = np.arange(lon_count)[:, None] * np.arange(freq)[None, :] % lon_count
    angle = phase * (2.0 * math.pi / lon_count)
    cosine = np.cos(angle)
    sine = np.where(2 * phase % lon_count == 0, 0.0, np.sin(angle))
    index = np.arange(freq)
    weight = np.where((index == 0) | (2 * index == lon_count), 1.0, 2.0) / lon_count
    table = np.zeros((lon_count, 2, bins), np.float64)
    table[:, 0, :freq] = cosine
    table[:, 1, :freq] = -sine
    table = table.reshape(lon_count, 2 * bins).astype(jnp.bfloat16)
    total = table.astype(np.float64).sum(axis=0, keepdims=True).astype(np.float32)
    scaled = np.zeros((2, bins), np.float32)
    scaled[:, :freq] = weight
    return table, total, scaled.reshape(1, 2 * bins)


def pixel_order(rows, cols):
    pixels = rows * cols
    index = np.arange(pixels)
    order = np.zeros((pixels, pixels), np.float32)
    order[index, index % rows * cols + index // rows] = 1.0
    return order.astype(jnp.bfloat16)


def place(index):
    pieces = lax.axis_size("lon")
    return (lax.div(index, pieces), lax.rem(index, pieces))


def own_index():
    return lax.axis_index("lat") * lax.axis_size("lon") + lax.axis_index("lon")


def drain(blocks, amount, semaphore):
    part = blocks.at[pl.ds(0, amount)]
    pltpu.make_async_copy(part, part, semaphore).wait()


def group_rows(size_ref, lanes, groups):
    group = lax.rem(lax.broadcasted_iota(jnp.int32, (1, lanes), 1), groups)
    start = jnp.zeros((1, lanes), jnp.int32)
    size = jnp.zeros((1, lanes), jnp.int32)
    for index in range(groups):
        start = start + jnp.where(group > index, size_ref[index], 0)
        size = size + jnp.where(group == index, size_ref[index], 0)
    return start, size


def membership(first, chan, start, size):
    channel = first + lax.broadcasted_iota(jnp.int32, (chan, start.shape[1]), 0)
    return (channel >= start) & (channel < start + size)


exact = functools.partial(
    lax.dot_general, precision=lax.Precision.HIGHEST, preferred_element_type=jnp.float32
)
OVER_FIRST = (((0,), (0,)), ((), ()))
OVER_LAST = (((1,), (1,)), ((), ()))


def block_body(
    devices, homes, sizes, freq, bins, rows, cols, chan_count, groups,
    size_hbm, band_hbm, x_hbm, order_hbm, coef_hbm, basis_hbm, table_hbm, total_hbm, weight_hbm, gain_hbm,
    win_hbm, wout_hbm,
    out_ref,
    size_ref, band_ref, x_ref, order_ref, coef_ref, basis_ref, table_ref, total_ref, weight_ref, gain_ref,
    win_ref, wout_ref,
    flat_ref, returned_ref, report_ref, reports_ref,
    kern_ref, wide_ref, spec_ref, prod_ref, corr_ref,
    load_sem, block_send_sem, block_recv_sem, report_send_sem, report_recv_sem,
    mixed_send_sem, mixed_recv_sem, local_sem, *part_refs,
):
    me = own_index()
    pieces = lax.axis_size("lon")
    bands = devices // pieces
    lat = bands * rows
    parts = len(sizes)
    chan = sum(sizes)
    offsets = [sum(sizes[:part]) for part in range(parts)]
    arrived_refs, mixed_refs = part_refs[:parts], part_refs[parts:]
    pixels = rows * cols
    band_count = basis_ref.shape[0] // TAPS
    own_home = lax.div(me * homes + devices - 1, devices)
    own_home = lax.rem(own_home, homes)
    is_home = lax.div(own_home * devices, homes) == me

    def device_of(home):
        return lax.div(home * devices, homes)

    barrier = pltpu.get_barrier_semaphore()

    def greet(step, carry):
        pl.semaphore_signal(
            barrier, inc=1, device_id=place(lax.rem(me + step, devices)), device_id_type=MESH
        )
        return carry

    loads = [
        pltpu.make_async_copy(source, target, load_sem.at[index])
        for index, (source, target) in enumerate(
            [
                (x_hbm, x_ref), (order_hbm, order_ref), (size_hbm, size_ref),
                (band_hbm, band_ref), (coef_hbm, coef_ref),
                (basis_hbm, basis_ref), (table_hbm, table_ref), (total_hbm, total_ref),
                (weight_hbm, weight_ref), (gain_hbm, gain_ref), (win_hbm, win_ref),
                (wout_hbm, wout_ref),
            ]
        )
    ]
    for load in loads[:2]:
        load.start()
    lax.fori_loop(1, devices, greet, 0)
    for load in loads[2:]:
        load.start()
    loads[0].wait()
    loads[1].wait()
    x = x_ref[...].reshape(pixels, chan_count)
    turned = lax.dot_general(
        x, order_ref[...], OVER_FIRST, preferred_element_type=jnp.float32
    ).astype(jnp.bfloat16)
    flat_ref[...] = jnp.zeros_like(flat_ref)
    flat_ref[:chan_count] = turned
    pl.semaphore_wait(barrier, devices - 1)

    def send_part(part):
        def send(step, carry):
            home = lax.rem(own_home + step, homes)
            target = device_of(home)
            first = pl.multiple_of(home * chan + offsets[part], SUB)

            @pl.when(target != me)
            def _():
                pltpu.make_async_remote_copy(
                    src_ref=flat_ref.at[pl.ds(first, sizes[part])],
                    dst_ref=arrived_refs[part].at[me],
                    send_sem=block_send_sem,
                    recv_sem=block_recv_sem.at[part],
                    device_id=place(target),
                    device_id_type=MESH,
                ).start()

            return carry

        lax.fori_loop(0, homes, send, 0)

    send_part(0)

    @pl.when(is_home)
    def _():
        for part in range(parts):
            first = pl.multiple_of(own_home * chan + offsets[part], SUB)
            pltpu.make_async_copy(
                flat_ref.at[pl.ds(first, sizes[part])], arrived_refs[part].at[me],
                local_sem.at[part],
            ).start()

    loads[2].wait()
    loads[3].wait()
    lane = lax.broadcasted_iota(jnp.int32, (pixels, 128), 0)
    slot = lax.broadcasted_iota(jnp.int32, (pixels, 128), 1)
    segment = (lane >= slot * cols) & (lane < (slot + 1) * cols)
    segment = jnp.where(segment, 1.0, 0.0).astype(jnp.bfloat16)

    def add_up(cells):
        return jnp.dot(cells, segment, preferred_element_type=jnp.float32)

    cells = flat_ref[...]
    means = add_up(cells) / cols
    near = means.astype(jnp.bfloat16)
    spread_out = lax.dot_general(near, segment, OVER_LAST, preferred_element_type=jnp.float32)
    offset = cells.astype(jnp.float32) - spread_out
    square = offset * offset
    high = square.astype(jnp.bfloat16)
    low = (square - high.astype(jnp.float32)).astype(jnp.bfloat16)
    shift = means - near.astype(jnp.float32)
    squares = jnp.maximum(add_up(high) + add_up(low) - cols * shift * shift, 0.0)
    start, size = group_rows(size_ref, 128, groups)
    member = jnp.where(
        membership(0, homes * chan, start, size)
        & (lax.broadcasted_iota(jnp.int32, (1, 128), 1) < groups),
        1.0, 0.0,
    )
    centre = exact(means, member, OVER_FIRST) / jnp.maximum(size, 1).astype(jnp.float32)
    offset = means - exact(member, centre, OVER_LAST)
    spread = exact(squares + cols * offset * offset, member, OVER_FIRST)
    lanes = report_ref.shape[1]
    rest = lanes - 2 * rows * groups
    place_of = lax.broadcasted_iota(jnp.int32, (1, rest), 1)
    numbers = jnp.zeros((1, rest), jnp.float32)
    for row in range(rows):
        numbers = jnp.where(place_of == row, band_ref[row].astype(jnp.float32), numbers)
    report = jnp.concatenate(
        [centre[row : row + 1, :groups] for row in range(rows)]
        + [spread[row : row + 1, :groups] for row in range(rows)]
        + [numbers],
        axis=1,
    )
    report_ref[...] = report
    reports_ref[me] = report

    def tell(step, carry):
        pltpu.make_async_remote_copy(
            src_ref=report_ref,
            dst_ref=reports_ref.at[me],
            send_sem=report_send_sem,
            recv_sem=report_recv_sem,
            device_id=place(lax.rem(me + step, devices)),
            device_id_type=MESH,
        ).start()
        return carry

    lax.fori_loop(1, devices, tell, 0)
    for part in range(1, parts):
        send_part(part)

    loads[4].wait()
    loads[5].wait()
    wanted = own_home * chan + lax.broadcasted_iota(jnp.int32, (chan, chan_count), 0)
    chosen = jnp.where(
        lax.broadcasted_iota(jnp.int32, (chan, chan_count), 1) == wanted, 1.0, 0.0
    )
    coef = exact(chosen, coef_ref[...], OVER_LAST)
    high = coef.astype(jnp.bfloat16).astype(jnp.float32)
    coef = jnp.concatenate([high, coef - high, high], axis=1).astype(jnp.bfloat16)
    blank = jnp.zeros((basis_ref.shape[1], bins - freq), jnp.float32)

    def generate(n, carry):
        basis = jnp.concatenate(
            [basis_ref[n, :, 0, :], blank, basis_ref[n, :, 1, :], blank], axis=1
        )
        high = basis.astype(jnp.bfloat16).astype(jnp.float32)
        both = jnp.concatenate([high, high, basis - high], axis=0).astype(jnp.bfloat16)
        made = jnp.dot(coef, both, preferred_element_type=jnp.float32)
        kern_ref[n, :chan] = made[:, :bins]
        kern_ref[n, chan:] = made[:, bins:]
        return carry

    lax.fori_loop(0, basis_ref.shape[0], generate, 0, unroll=3)
    for load in loads[6:]:
        load.wait()
    drain(reports_ref, devices - 1, report_send_sem)
    drain(reports_ref, devices - 1, report_recv_sem)

    @pl.when(is_home)
    def _():
        start, size = group_rows(size_ref, lanes, groups)
        amount = size.astype(jnp.float32) * cols
        lane = lax.broadcasted_iota(jnp.int32, (1, lanes), 1)
        seen = []
        for band in range(bands):
            report = reports_ref[band * pieces : (band + 1) * pieces, 0]
            centre = jnp.sum(report, axis=0, keepdims=True) / pieces
            offset = report - centre
            between = amount * jnp.sum(offset * offset, axis=0, keepdims=True)
            within = jnp.sum(report, axis=0, keepdims=True)
            seen.append((report, centre, between, within))
        band_of = []
        for band in range(bands):
            for row in range(rows):
                mark = lane == 2 * rows * groups + row
                number = jnp.sum(jnp.where(mark, seen[band][0][:1], 0.0)).astype(jnp.int32)
                band_of.append(jnp.clip(number, 0, band_count - 1))
        for part in range(parts):
            size_of, arrived_ref, mixed_ref = sizes[part], arrived_refs[part], mixed_refs[part]
            span = lat * size_of
            pltpu.make_async_copy(
                flat_ref.at[pl.ds(0, size_of)], arrived_ref.at[me], local_sem.at[part]
            ).wait()
            drain(arrived_ref, devices - 1, block_recv_sem.at[part])
            member = membership(own_home * chan + offsets[part], size_of, start, size)
            for band in range(bands):
                for piece in range(pieces):
                    cells = arrived_ref[band * pieces + piece].astype(jnp.float32)
                    for row in range(rows):
                        at = (band * rows + row) * size_of
                        wide_ref[at : at + size_of, piece * cols : (piece + 1) * cols] = cells[
                            :, row * cols : (row + 1) * cols
                        ]
            raw = jnp.dot(
                wide_ref[:span].astype(jnp.bfloat16), table_ref[...],
                preferred_element_type=jnp.float32,
            )
            for band in range(bands):
                _, centre, between, within = seen[band]
                for row in range(rows):
                    low, high = row * groups, (rows + row) * groups
                    here = member & (lane >= low) & (lane < low + groups)
                    there = member & (lane >= high) & (lane < high + groups)

                    def pick(mask, cells):
                        return jnp.sum(jnp.where(mask, cells, 0.0), axis=1, keepdims=True)

                    square = pick(here, between) + pick(there, within)
                    count = pick(here, amount) * pieces
                    mean = pick(here, centre)
                    scale = lax.rsqrt(square / jnp.maximum(count, 1.0) + EPSILON)
                    at = (band * rows + row) * size_of
                    spec_ref[at : at + size_of] = (raw[at : at + size_of] - mean * total_ref[...]) * scale
            for row in range(lat):
                real = jnp.zeros((size_of, bins), jnp.float32)
                imag = jnp.zeros((size_of, bins), jnp.float32)
                for tap in range(TAPS):
                    source = row + tap - HALO
                    if source < 0 or source >= lat:
                        continue
                    at = source * size_of
                    spec_real = spec_ref[at : at + size_of, :bins]
                    spec_imag = spec_ref[at : at + size_of, bins:]
                    index = band_of[row] * TAPS + tap
                    at = offsets[part]
                    kern_real = kern_ref[index, at : at + size_of]
                    kern_imag = kern_ref[index, chan + at : chan + at + size_of]
                    real = real + kern_real * spec_real - kern_imag * spec_imag
                    imag = imag + kern_real * spec_imag + kern_imag * spec_real
                prod_ref[row * size_of : (row + 1) * size_of, :bins] = real
                prod_ref[row * size_of : (row + 1) * size_of, bins:] = imag
            corr_ref[:span] = lax.dot_general(
                (prod_ref[:span] * weight_ref[...]).astype(jnp.bfloat16),
                table_ref[...],
                OVER_LAST,
                preferred_element_type=jnp.float32,
            )
            for band in range(bands):
                for piece in range(pieces):
                    pieces_of = []
                    for row in range(rows):
                        at = (band * rows + row) * size_of
                        pieces_of.append(
                            corr_ref[at : at + size_of, piece * cols : (piece + 1) * cols]
                        )
                    device = band * pieces + piece
                    cells = arrived_ref[device].astype(jnp.float32)
                    mixed_ref[device] = (
                        cells + jnp.concatenate(pieces_of, axis=1)
                    ).astype(jnp.bfloat16)
            first = pl.multiple_of(own_home * chan + offsets[part], SUB)

            def give(step, carry):
                target = step

                @pl.when(target != me)
                def _():
                    pltpu.make_async_remote_copy(
                        src_ref=mixed_ref.at[target],
                        dst_ref=returned_ref.at[pl.ds(first, size_of)],
                        send_sem=mixed_send_sem,
                        recv_sem=mixed_recv_sem,
                        device_id=place(target),
                        device_id_type=MESH,
                    ).start()

                return carry

            lax.fori_loop(0, devices, give, 0)
            pltpu.make_async_copy(
                mixed_ref.at[me], returned_ref.at[pl.ds(first, size_of)], local_sem.at[part]
            ).start()
        for part in range(parts):
            pltpu.make_async_copy(
                mixed_refs[part].at[me], returned_ref.at[pl.ds(0, sizes[part])],
                local_sem.at[part],
            ).wait()
            drain(mixed_refs[part], devices - 1, mixed_send_sem)
        drain(flat_ref, (homes - 1) * chan, block_send_sem)
        drain(returned_ref, (homes - 1) * chan, mixed_recv_sem)

    @pl.when(jnp.logical_not(is_home))
    def _():
        drain(flat_ref, homes * chan, block_send_sem)
        drain(returned_ref, homes * chan, mixed_recv_sem)

    step = pixels
    for at in range(0, pixels, step):
        inputs = lax.dot_general(
            order_ref[at : at + step, :], returned_ref[...], OVER_LAST,
            preferred_element_type=jnp.float32,
        )[:, :chan_count]
        centre = jnp.mean(inputs, axis=-1, keepdims=True)
        spread = jnp.mean((inputs - centre) ** 2, axis=-1, keepdims=True)
        normalised = (
            (inputs - centre) * lax.rsqrt(spread + EPSILON) * gain_ref[...].reshape(1, chan_count)
        ).astype(jnp.bfloat16)
        hidden = jnp.dot(normalised, win_ref[...], preferred_element_type=jnp.float32)
        hidden = (0.5 * hidden * (1.0 + lax.erf(hidden * math.sqrt(0.5)))).astype(jnp.bfloat16)
        result = inputs + lax.dot_general(
            hidden, wout_ref[...], OVER_LAST, preferred_element_type=jnp.float32
        )
        out_ref[at // rows : (at + step) // rows] = result.astype(jnp.bfloat16).reshape(
            step // rows, rows, chan_count
        )


def per_device(fields, group_size, band_of_row, basis_spectra, basis_coef, mlp_gain, w_in, w_out):
    row_count, col_count, chan_count = fields.shape
    pieces = lax.axis_size("lon")
    bands = lax.axis_size("lat")
    devices = pieces * bands
    lon_count = col_count * pieces
    lat_count = row_count * bands
    freq_count = lon_count // 2 + 1
    groups = group_size.shape[0]
    pixels = row_count * col_count
    chan = round_up(-(-chan_count // devices), SUB)
    homes = -(-chan_count // chan)
    sizes = [SUB] + [chan - SUB] * (chan > SUB)
    parts = len(sizes)
    tallest = lat_count * max(sizes)
    bins = round_up(freq_count, 128)
    band_count, _, basis_count = basis_spectra.shape[:3]
    hidden = w_in.shape[1]
    lanes = round_up((2 * groups + 1) * row_count, 128)
    table, total, weight = dft_tables(lon_count, bins)
    basis = basis_spectra.reshape(band_count * TAPS, basis_count, 2, freq_count)
    f32, bf16 = jnp.float32, jnp.bfloat16
    scalars = [group_size, band_of_row]
    operands = [
        (jnp.transpose(fields, (1, 0, 2)), bf16),
        (pixel_order(row_count, col_count), bf16),
        (basis_coef.T, f32),
        (basis, f32),
        (table, bf16),
        (total, f32),
        (weight, f32),
        (mlp_gain, f32),
        (w_in, bf16),
        (w_out.T, bf16),
    ]
    out = pl.pallas_call(
        functools.partial(
            block_body, devices, homes, sizes, freq_count, bins, row_count, col_count,
            chan_count, groups,
        ),
        out_shape=jax.ShapeDtypeStruct((col_count, row_count, chan_count), bf16),
        in_specs=[HBM] * (len(scalars) + len(operands)),
        out_specs=VMEM,
        scratch_shapes=[pltpu.SMEM(array.shape, jnp.int32) for array in scalars]
        + [pltpu.VMEM(array.shape, kind) for array, kind in operands]
        + [
            pltpu.VMEM((homes * chan, pixels), bf16),
            pltpu.VMEM((homes * chan, pixels), bf16),
            pltpu.VMEM((1, lanes), f32),
            pltpu.VMEM((devices, 1, lanes), f32),
            pltpu.VMEM((band_count * TAPS, 2 * chan, bins), f32),
            pltpu.VMEM((tallest, lon_count), f32),
            pltpu.VMEM((tallest, 2 * bins), f32),
            pltpu.VMEM((tallest, 2 * bins), f32),
            pltpu.VMEM((tallest, lon_count), f32),
            DMA((len(scalars) + len(operands),)),
            DMA,
            DMA((parts,)),
            DMA,
            DMA,
            DMA,
            DMA,
            DMA((parts,)),
        ]
        + [pltpu.VMEM((devices, size, pixels), bf16) for size in sizes] * 2,
        compiler_params=pltpu.CompilerParams(
            collective_id=0, has_side_effects=True, vmem_limit_bytes=60 * 1024 * 1024
        ),
    )(*scalars, *[array for array, _ in operands])
    return jnp.transpose(out, (1, 0, 2))


def solution(mesh):
    placed = (P("lat", "lon", None), P(), P("lat"), P(), P(), P(), P(), P())
    return jax.shard_map(
        per_device, mesh=mesh, in_specs=placed, out_specs=P("lat", "lon", None), check_vma=False
    )
```

```python
import functools
import math

import jax
import jax.numpy as jnp
import numpy as np
from jax import lax
from jax.experimental import pallas as pl
from jax.experimental.pallas import tpu as pltpu
from jax.sharding import PartitionSpec as P

HALO = 4
TAPS = 2 * HALO + 1
EPSILON = 1e-05
SUB = 8
VMEM = pl.BlockSpec(memory_space=pltpu.VMEM)
HBM = pl.BlockSpec(memory_space=pltpu.HBM)
MESH = pl.DeviceIdType.MESH
DMA = pltpu.SemaphoreType.DMA


def round_up(value, step):
    return -(-value // step) * step


def dft_tables(lon_count, bins):
    freq = lon_count // 2 + 1
    phase = np.arange(lon_count)[:, None] * np.arange(freq)[None, :] % lon_count
    angle = phase * (2.0 * math.pi / lon_count)
    cosine = np.cos(angle)
    sine = np.where(2 * phase % lon_count == 0, 0.0, np.sin(angle))
    index = np.arange(freq)
    weight = np.where((index == 0) | (2 * index == lon_count), 1.0, 2.0) / lon_count
    table = np.zeros((lon_count, 2, bins), np.float64)
    table[:, 0, :freq] = cosine
    table[:, 1, :freq] = -sine
    table = table.reshape(lon_count, 2 * bins).astype(jnp.bfloat16)
    total = table.astype(np.float64).sum(axis=0, keepdims=True).astype(np.float32)
    scaled = np.zeros((2, bins), np.float32)
    scaled[:, :freq] = weight
    return table, total, scaled.reshape(1, 2 * bins)


def pixel_order(rows, cols):
    pixels = rows * cols
    index = np.arange(pixels)
    order = np.zeros((pixels, pixels), np.float32)
    order[index, index % rows * cols + index // rows] = 1.0
    return order.astype(jnp.bfloat16)


def place(index):
    pieces = lax.axis_size("lon")
    return (lax.div(index, pieces), lax.rem(index, pieces))


def own_index():
    return lax.axis_index("lat") * lax.axis_size("lon") + lax.axis_index("lon")


def drain(blocks, amount, semaphore):
    part = blocks.at[pl.ds(0, amount)]
    pltpu.make_async_copy(part, part, semaphore).wait()


def group_rows(size_ref, lanes, groups):
    group = lax.rem(lax.broadcasted_iota(jnp.int32, (1, lanes), 1), groups)
    start = jnp.zeros((1, lanes), jnp.int32)
    size = jnp.zeros((1, lanes), jnp.int32)
    for index in range(groups):
        start = start + jnp.where(group > index, size_ref[index], 0)
        size = size + jnp.where(group == index, size_ref[index], 0)
    return start, size


def membership(first, chan, start, size):
    channel = first + lax.broadcasted_iota(jnp.int32, (chan, start.shape[1]), 0)
    return (channel >= start) & (channel < start + size)


exact = functools.partial(
    lax.dot_general, precision=lax.Precision.HIGHEST, preferred_element_type=jnp.float32
)
OVER_FIRST = (((0,), (0,)), ((), ()))
OVER_LAST = (((1,), (1,)), ((), ()))


def block_body(
    devices, homes, sizes, freq, bins, rows, cols, chan_count, groups,
    size_hbm, band_hbm, x_hbm, order_hbm, coef_hbm, basis_hbm, table_hbm, total_hbm, weight_hbm, gain_hbm,
    win_hbm, wout_hbm,
    out_ref,
    size_ref, band_ref, x_ref, order_ref, coef_ref, basis_ref, table_ref, total_ref, weight_ref, gain_ref,
    win_ref, wout_ref,
    flat_ref, returned_ref, report_ref, reports_ref,
    kern_ref, wide_ref, spec_ref, prod_ref, corr_ref, rest_ref,
    load_sem, block_send_sem, block_recv_sem, report_send_sem, report_recv_sem,
    mixed_send_sem, mixed_recv_sem, local_sem, *part_refs,
):
    me = own_index()
    pieces = lax.axis_size("lon")
    bands = devices // pieces
    lat = bands * rows
    parts = len(sizes)
    chan = sum(sizes)
    offsets = [sum(sizes[:part]) for part in range(parts)]
    arrived_refs, mixed_refs = part_refs[:parts], part_refs[parts:]
    pixels = rows * cols
    band_count = basis_ref.shape[0] // TAPS
    own_home = lax.div(me * homes + devices - 1, devices)
    own_home = lax.rem(own_home, homes)
    is_home = lax.div(own_home * devices, homes) == me

    def device_of(home):
        return lax.div(home * devices, homes)

    barrier = pltpu.get_barrier_semaphore()

    def greet(step, carry):
        pl.semaphore_signal(
            barrier, inc=1, device_id=place(lax.rem(me + step, devices)), device_id_type=MESH
        )
        return carry

    loads = [
        pltpu.make_async_copy(source, target, load_sem.at[index])
        for index, (source, target) in enumerate(
            [
                (x_hbm, x_ref), (order_hbm, order_ref), (size_hbm, size_ref),
                (band_hbm, band_ref), (coef_hbm, coef_ref),
                (basis_hbm, basis_ref), (table_hbm, table_ref), (total_hbm, total_ref),
                (weight_hbm, weight_ref), (gain_hbm, gain_ref), (win_hbm, win_ref),
                (wout_hbm, wout_ref),
            ]
        )
    ]
    for load in loads[:2]:
        load.start()
    lax.fori_loop(1, devices, greet, 0)
    for load in loads[2:]:
        load.start()
    loads[0].wait()
    loads[1].wait()
    x = x_ref[...].reshape(pixels, chan_count)
    turned = lax.dot_general(
        x, order_ref[...], OVER_FIRST, preferred_element_type=jnp.float32
    ).astype(jnp.bfloat16)
    flat_ref[...] = jnp.zeros_like(flat_ref)
    flat_ref[:chan_count] = turned
    pl.semaphore_wait(barrier, devices - 1)

    def send_part(part):
        def send(step, carry):
            home = lax.rem(own_home + step, homes)
            target = device_of(home)
            first = pl.multiple_of(home * chan + offsets[part], SUB)

            @pl.when(target != me)
            def _():
                pltpu.make_async_remote_copy(
                    src_ref=flat_ref.at[pl.ds(first, sizes[part])],
                    dst_ref=arrived_refs[part].at[me],
                    send_sem=block_send_sem,
                    recv_sem=block_recv_sem.at[part],
                    device_id=place(target),
                    device_id_type=MESH,
                ).start()

            return carry

        lax.fori_loop(0, homes, send, 0)

    send_part(0)

    @pl.when(is_home)
    def _():
        for part in range(parts):
            first = pl.multiple_of(own_home * chan + offsets[part], SUB)
            pltpu.make_async_copy(
                flat_ref.at[pl.ds(first, sizes[part])], arrived_refs[part].at[me],
                local_sem.at[part],
            ).start()

    loads[2].wait()
    loads[3].wait()
    lane = lax.broadcasted_iota(jnp.int32, (pixels, 128), 0)
    slot = lax.broadcasted_iota(jnp.int32, (pixels, 128), 1)
    segment = (lane >= slot * cols) & (lane < (slot + 1) * cols)
    segment = jnp.where(segment, 1.0, 0.0).astype(jnp.bfloat16)

    def add_up(cells):
        return jnp.dot(cells, segment, preferred_element_type=jnp.float32)

    cells = flat_ref[...]
    means = add_up(cells) / cols
    near = means.astype(jnp.bfloat16)
    spread_out = lax.dot_general(near, segment, OVER_LAST, preferred_element_type=jnp.float32)
    offset = cells.astype(jnp.float32) - spread_out
    square = offset * offset
    high = square.astype(jnp.bfloat16)
    low = (square - high.astype(jnp.float32)).astype(jnp.bfloat16)
    shift = means - near.astype(jnp.float32)
    squares = jnp.maximum(add_up(high) + add_up(low) - cols * shift * shift, 0.0)
    start, size = group_rows(size_ref, 128, groups)
    member = jnp.where(
        membership(0, homes * chan, start, size)
        & (lax.broadcasted_iota(jnp.int32, (1, 128), 1) < groups),
        1.0, 0.0,
    )
    centre = exact(means, member, OVER_FIRST) / jnp.maximum(size, 1).astype(jnp.float32)
    offset = means - exact(member, centre, OVER_LAST)
    spread = exact(squares + cols * offset * offset, member, OVER_FIRST)
    lanes = report_ref.shape[1]
    rest = lanes - 2 * rows * groups
    place_of = lax.broadcasted_iota(jnp.int32, (1, rest), 1)
    numbers = jnp.zeros((1, rest), jnp.float32)
    for row in range(rows):
        numbers = jnp.where(place_of == row, band_ref[row].astype(jnp.float32), numbers)
    report = jnp.concatenate(
        [centre[row : row + 1, :groups] for row in range(rows)]
        + [spread[row : row + 1, :groups] for row in range(rows)]
        + [numbers],
        axis=1,
    )
    report_ref[...] = report
    reports_ref[me] = report

    def tell(step, carry):
        pltpu.make_async_remote_copy(
            src_ref=report_ref,
            dst_ref=reports_ref.at[me],
            send_sem=report_send_sem,
            recv_sem=report_recv_sem,
            device_id=place(lax.rem(me + step, devices)),
            device_id_type=MESH,
        ).start()
        return carry

    lax.fori_loop(1, devices, tell, 0)
    for part in range(1, parts):
        send_part(part)

    loads[4].wait()
    loads[5].wait()
    wanted = own_home * chan + lax.broadcasted_iota(jnp.int32, (chan, chan_count), 0)
    chosen = jnp.where(
        lax.broadcasted_iota(jnp.int32, (chan, chan_count), 1) == wanted, 1.0, 0.0
    )
    coef = exact(chosen, coef_ref[...], OVER_LAST)
    high = coef.astype(jnp.bfloat16).astype(jnp.float32)
    coef = jnp.concatenate([high, coef - high, high], axis=1).astype(jnp.bfloat16)
    blank = jnp.zeros((basis_ref.shape[1], bins - freq), jnp.float32)

    def generate(n, carry):
        basis = jnp.concatenate(
            [basis_ref[n, :, 0, :], blank, basis_ref[n, :, 1, :], blank], axis=1
        )
        high = basis.astype(jnp.bfloat16).astype(jnp.float32)
        both = jnp.concatenate([high, high, basis - high], axis=0).astype(jnp.bfloat16)
        made = jnp.dot(coef, both, preferred_element_type=jnp.float32)
        kern_ref[n, :chan] = made[:, :bins]
        kern_ref[n, chan:] = made[:, bins:]
        return carry

    lax.fori_loop(0, basis_ref.shape[0], generate, 0, unroll=3)
    for load in loads[6:]:
        load.wait()
    rest = win_ref.shape[1] % 256
    rest = rest if rest <= SUB else 0
    whole = win_ref.shape[1] - rest
    if rest:
        for index, weights in enumerate((win_ref, wout_ref)):
            tail = weights[:, whole:].astype(jnp.float32)
            tail = jnp.concatenate([tail, jnp.zeros((chan_count, 128 - rest), jnp.float32)], axis=1)
            rest_ref[index * SUB : (index + 1) * SUB] = tail.T[:SUB]
    drain(reports_ref, devices - 1, report_send_sem)
    drain(reports_ref, devices - 1, report_recv_sem)

    @pl.when(is_home)
    def _():
        start, size = group_rows(size_ref, lanes, groups)
        amount = size.astype(jnp.float32) * cols
        lane = lax.broadcasted_iota(jnp.int32, (1, lanes), 1)
        seen = []
        for band in range(bands):
            report = reports_ref[band * pieces : (band + 1) * pieces, 0]
            centre = jnp.sum(report, axis=0, keepdims=True) / pieces
            offset = report - centre
            between = amount * jnp.sum(offset * offset, axis=0, keepdims=True)
            within = jnp.sum(report, axis=0, keepdims=True)
            seen.append((report, centre, between, within))
        band_of = []
        for band in range(bands):
            for row in range(rows):
                mark = lane == 2 * rows * groups + row
                number = jnp.sum(jnp.where(mark, seen[band][0][:1], 0.0)).astype(jnp.int32)
                band_of.append(jnp.clip(number, 0, band_count - 1))
        for part in range(parts):
            size_of, arrived_ref, mixed_ref = sizes[part], arrived_refs[part], mixed_refs[part]
            span = lat * size_of
            pltpu.make_async_copy(
                flat_ref.at[pl.ds(0, size_of)], arrived_ref.at[me], local_sem.at[part]
            ).wait()
            drain(arrived_ref, devices - 1, block_recv_sem.at[part])
            member = membership(own_home * chan + offsets[part], size_of, start, size)
            for band in range(bands):
                for piece in range(pieces):
                    cells = arrived_ref[band * pieces + piece].astype(jnp.float32)
                    for row in range(rows):
                        at = (band * rows + row) * size_of
                        wide_ref[at : at + size_of, piece * cols : (piece + 1) * cols] = cells[
                            :, row * cols : (row + 1) * cols
                        ]
            raw = jnp.dot(
                wide_ref[:span].astype(jnp.bfloat16), table_ref[...],
                preferred_element_type=jnp.float32,
            )
            for band in range(bands):
                _, centre, between, within = seen[band]
                for row in range(rows):
                    low, high = row * groups, (rows + row) * groups
                    here = member & (lane >= low) & (lane < low + groups)
                    there = member & (lane >= high) & (lane < high + groups)

                    def pick(mask, cells):
                        return jnp.sum(jnp.where(mask, cells, 0.0), axis=1, keepdims=True)

                    square = pick(here, between) + pick(there, within)
                    count = pick(here, amount) * pieces
                    mean = pick(here, centre)
                    scale = lax.rsqrt(square / jnp.maximum(count, 1.0) + EPSILON)
                    at = (band * rows + row) * size_of
                    spec_ref[at : at + size_of] = (raw[at : at + size_of] - mean * total_ref[...]) * scale
            for row in range(lat):
                real = jnp.zeros((size_of, bins), jnp.float32)
                imag = jnp.zeros((size_of, bins), jnp.float32)
                for tap in range(TAPS):
                    source = row + tap - HALO
                    if source < 0 or source >= lat:
                        continue
                    at = source * size_of
                    spec_real = spec_ref[at : at + size_of, :bins]
                    spec_imag = spec_ref[at : at + size_of, bins:]
                    index = band_of[row] * TAPS + tap
                    at = offsets[part]
                    kern_real = kern_ref[index, at : at + size_of]
                    kern_imag = kern_ref[index, chan + at : chan + at + size_of]
                    real = real + kern_real * spec_real - kern_imag * spec_imag
                    imag = imag + kern_real * spec_imag + kern_imag * spec_real
                prod_ref[row * size_of : (row + 1) * size_of, :bins] = real
                prod_ref[row * size_of : (row + 1) * size_of, bins:] = imag
            corr_ref[:span] = lax.dot_general(
                (prod_ref[:span] * weight_ref[...]).astype(jnp.bfloat16),
                table_ref[...],
                OVER_LAST,
                preferred_element_type=jnp.float32,
            )
            for band in range(bands):
                for piece in range(pieces):
                    pieces_of = []
                    for row in range(rows):
                        at = (band * rows + row) * size_of
                        pieces_of.append(
                            corr_ref[at : at + size_of, piece * cols : (piece + 1) * cols]
                        )
                    device = band * pieces + piece
                    cells = arrived_ref[device].astype(jnp.float32)
                    mixed_ref[device] = (
                        cells + jnp.concatenate(pieces_of, axis=1)
                    ).astype(jnp.bfloat16)
            first = pl.multiple_of(own_home * chan + offsets[part], SUB)

            def give(step, carry):
                target = step

                @pl.when(target != me)
                def _():
                    pltpu.make_async_remote_copy(
                        src_ref=mixed_ref.at[target],
                        dst_ref=returned_ref.at[pl.ds(first, size_of)],
                        send_sem=mixed_send_sem,
                        recv_sem=mixed_recv_sem,
                        device_id=place(target),
                        device_id_type=MESH,
                    ).start()

                return carry

            lax.fori_loop(0, devices, give, 0)
            pltpu.make_async_copy(
                mixed_ref.at[me], returned_ref.at[pl.ds(first, size_of)], local_sem.at[part]
            ).start()
        for part in range(parts):
            pltpu.make_async_copy(
                mixed_refs[part].at[me], returned_ref.at[pl.ds(0, sizes[part])],
                local_sem.at[part],
            ).wait()
            drain(mixed_refs[part], devices - 1, mixed_send_sem)
        drain(flat_ref, (homes - 1) * chan, block_send_sem)
        drain(returned_ref, (homes - 1) * chan, mixed_recv_sem)

    @pl.when(jnp.logical_not(is_home))
    def _():
        drain(flat_ref, homes * chan, block_send_sem)
        drain(returned_ref, homes * chan, mixed_recv_sem)

    def gelu(hidden):
        return (0.5 * hidden * (1.0 + lax.erf(hidden * math.sqrt(0.5)))).astype(jnp.bfloat16)

    step = pixels
    for at in range(0, pixels, step):
        inputs = lax.dot_general(
            order_ref[at : at + step, :], returned_ref[...], OVER_LAST,
            preferred_element_type=jnp.float32,
        )[:, :chan_count]
        centre = jnp.mean(inputs, axis=-1, keepdims=True)
        spread = jnp.mean((inputs - centre) ** 2, axis=-1, keepdims=True)
        normalised = (
            (inputs - centre) * lax.rsqrt(spread + EPSILON) * gain_ref[...].reshape(1, chan_count)
        ).astype(jnp.bfloat16)
        result = inputs
        for unit in range(rest):
            column = rest_ref[unit : unit + 1]
            hidden = jnp.sum(normalised.astype(jnp.float32) * column, axis=1, keepdims=True)
            result = result + gelu(hidden).astype(jnp.float32) * rest_ref[SUB + unit : SUB + unit + 1]
        hidden = jnp.dot(normalised, win_ref[:, :whole], preferred_element_type=jnp.float32)
        result = result + lax.dot_general(
            gelu(hidden), wout_ref[:, :whole], OVER_LAST, preferred_element_type=jnp.float32
        )
        out_ref[at // rows : (at + step) // rows] = result.astype(jnp.bfloat16).reshape(
            step // rows, rows, chan_count
        )


def per_device(fields, group_size, band_of_row, basis_spectra, basis_coef, mlp_gain, w_in, w_out):
    row_count, col_count, chan_count = fields.shape
    pieces = lax.axis_size("lon")
    bands = lax.axis_size("lat")
    devices = pieces * bands
    lon_count = col_count * pieces
    lat_count = row_count * bands
    freq_count = lon_count // 2 + 1
    groups = group_size.shape[0]
    pixels = row_count * col_count
    chan = round_up(-(-chan_count // devices), SUB)
    homes = -(-chan_count // chan)
    sizes = [SUB] + [chan - SUB] * (chan > SUB)
    parts = len(sizes)
    tallest = lat_count * max(sizes)
    bins = round_up(freq_count, 128)
    band_count, _, basis_count = basis_spectra.shape[:3]
    hidden = w_in.shape[1]
    lanes = round_up((2 * groups + 1) * row_count, 128)
    table, total, weight = dft_tables(lon_count, bins)
    basis = basis_spectra.reshape(band_count * TAPS, basis_count, 2, freq_count)
    f32, bf16 = jnp.float32, jnp.bfloat16
    scalars = [group_size, band_of_row]
    operands = [
        (jnp.transpose(fields, (1, 0, 2)), bf16),
        (pixel_order(row_count, col_count), bf16),
        (basis_coef.T, f32),
        (basis, f32),
        (table, bf16),
        (total, f32),
        (weight, f32),
        (mlp_gain, f32),
        (w_in, bf16),
        (w_out.T, bf16),
    ]
    out = pl.pallas_call(
        functools.partial(
            block_body, devices, homes, sizes, freq_count, bins, row_count, col_count,
            chan_count, groups,
        ),
        out_shape=jax.ShapeDtypeStruct((col_count, row_count, chan_count), bf16),
        in_specs=[HBM] * (len(scalars) + len(operands)),
        out_specs=VMEM,
        scratch_shapes=[pltpu.SMEM(array.shape, jnp.int32) for array in scalars]
        + [pltpu.VMEM(array.shape, kind) for array, kind in operands]
        + [
            pltpu.VMEM((homes * chan, pixels), bf16),
            pltpu.VMEM((homes * chan, pixels), bf16),
            pltpu.VMEM((1, lanes), f32),
            pltpu.VMEM((devices, 1, lanes), f32),
            pltpu.VMEM((band_count * TAPS, 2 * chan, bins), f32),
            pltpu.VMEM((tallest, lon_count), f32),
            pltpu.VMEM((tallest, 2 * bins), f32),
            pltpu.VMEM((tallest, 2 * bins), f32),
            pltpu.VMEM((tallest, lon_count), f32),
            pltpu.VMEM((2 * SUB, chan_count), f32),
            DMA((len(scalars) + len(operands),)),
            DMA,
            DMA((parts,)),
            DMA,
            DMA,
            DMA,
            DMA,
            DMA((parts,)),
        ]
        + [pltpu.VMEM((devices, size, pixels), bf16) for size in sizes] * 2,
        compiler_params=pltpu.CompilerParams(
            collective_id=0, has_side_effects=True, vmem_limit_bytes=60 * 1024 * 1024
        ),
    )(*scalars, *[array for array, _ in operands])
    return jnp.transpose(out, (1, 0, 2))


def solution(mesh):
    placed = (P("lat", "lon", None), P(), P("lat"), P(), P(), P(), P(), P())
    return jax.shard_map(
        per_device, mesh=mesh, in_specs=placed, out_specs=P("lat", "lon", None), check_vma=False
    )
```

```python
import functools
import math

import jax
import jax.numpy as jnp
import numpy as np
from jax import lax
from jax.experimental import pallas as pl
from jax.experimental.pallas import tpu as pltpu
from jax.sharding import PartitionSpec as P

HALO = 4
TAPS = 2 * HALO + 1
EPSILON = 1e-05
SUB = 8
VMEM = pl.BlockSpec(memory_space=pltpu.VMEM)
HBM = pl.BlockSpec(memory_space=pltpu.HBM)
MESH = pl.DeviceIdType.MESH
DMA = pltpu.SemaphoreType.DMA


def round_up(value, step):
    return -(-value // step) * step


def dft_tables(lon_count, bins):
    freq = lon_count // 2 + 1
    phase = np.arange(lon_count)[:, None] * np.arange(freq)[None, :] % lon_count
    angle = phase * (2.0 * math.pi / lon_count)
    cosine = np.cos(angle)
    sine = np.where(2 * phase % lon_count == 0, 0.0, np.sin(angle))
    index = np.arange(freq)
    weight = np.where((index == 0) | (2 * index == lon_count), 1.0, 2.0) / lon_count
    table = np.zeros((lon_count, 2, bins), np.float64)
    table[:, 0, :freq] = cosine
    table[:, 1, :freq] = -sine
    table = table.reshape(lon_count, 2 * bins).astype(jnp.bfloat16)
    total = table.astype(np.float64).sum(axis=0, keepdims=True).astype(np.float32)
    scaled = np.zeros((2, bins), np.float32)
    scaled[:, :freq] = weight
    return table, total, scaled.reshape(1, 2 * bins)


def pixel_order(rows, cols):
    pixels = rows * cols
    index = np.arange(pixels)
    order = np.zeros((pixels, pixels), np.float32)
    order[index, index % rows * cols + index // rows] = 1.0
    return order.astype(jnp.bfloat16)


def place(index):
    pieces = lax.axis_size("lon")
    return (lax.div(index, pieces), lax.rem(index, pieces))


def own_index():
    return lax.axis_index("lat") * lax.axis_size("lon") + lax.axis_index("lon")


def drain(blocks, amount, semaphore):
    part = blocks.at[pl.ds(0, amount)]
    pltpu.make_async_copy(part, part, semaphore).wait()


def group_rows(size_ref, lanes, groups):
    group = lax.rem(lax.broadcasted_iota(jnp.int32, (1, lanes), 1), groups)
    start = jnp.zeros((1, lanes), jnp.int32)
    size = jnp.zeros((1, lanes), jnp.int32)
    for index in range(groups):
        start = start + jnp.where(group > index, size_ref[index], 0)
        size = size + jnp.where(group == index, size_ref[index], 0)
    return start, size


def membership(first, chan, start, size):
    channel = first + lax.broadcasted_iota(jnp.int32, (chan, start.shape[1]), 0)
    return (channel >= start) & (channel < start + size)


exact = functools.partial(
    lax.dot_general, precision=lax.Precision.HIGHEST, preferred_element_type=jnp.float32
)
OVER_FIRST = (((0,), (0,)), ((), ()))
OVER_LAST = (((1,), (1,)), ((), ()))


def block_body(
    devices, homes, sizes, freq, bins, rows, cols, chan_count, groups,
    size_hbm, band_hbm, x_hbm, order_hbm, coef_hbm, basis_hbm, table_hbm, total_hbm, weight_hbm, gain_hbm,
    win_hbm, wout_hbm,
    out_ref,
    size_ref, band_ref, x_ref, order_ref, coef_ref, basis_ref, table_ref, total_ref, weight_ref, gain_ref,
    win_ref, wout_ref,
    flat_ref, returned_ref, report_ref, reports_ref,
    kern_ref, wide_ref, spec_ref, prod_ref, corr_ref, rest_ref,
    load_sem, block_send_sem, block_recv_sem, report_send_sem, report_recv_sem,
    mixed_send_sem, mixed_recv_sem, local_sem, *part_refs,
):
    me = own_index()
    pieces = lax.axis_size("lon")
    bands = devices // pieces
    lat = bands * rows
    parts = len(sizes)
    chan = sum(sizes)
    offsets = [sum(sizes[:part]) for part in range(parts)]
    arrived_refs, mixed_refs = part_refs[:parts], part_refs[parts:]
    pixels = rows * cols
    band_count = basis_ref.shape[0] // TAPS
    own_home = lax.div(me * homes + devices - 1, devices)
    own_home = lax.rem(own_home, homes)
    is_home = lax.div(own_home * devices, homes) == me

    def device_of(home):
        return lax.div(home * devices, homes)

    barrier = pltpu.get_barrier_semaphore()

    def greet(step, carry):
        pl.semaphore_signal(
            barrier, inc=1, device_id=place(lax.rem(me + step, devices)), device_id_type=MESH
        )
        return carry

    loads = [
        pltpu.make_async_copy(source, target, load_sem.at[index])
        for index, (source, target) in enumerate(
            [
                (x_hbm, x_ref), (order_hbm, order_ref), (size_hbm, size_ref),
                (band_hbm, band_ref), (coef_hbm, coef_ref),
                (basis_hbm, basis_ref), (table_hbm, table_ref), (total_hbm, total_ref),
                (weight_hbm, weight_ref), (gain_hbm, gain_ref), (win_hbm, win_ref),
                (wout_hbm, wout_ref),
            ]
        )
    ]
    for load in loads[:2]:
        load.start()
    lax.fori_loop(1, devices, greet, 0)
    for load in loads[2:]:
        load.start()
    loads[0].wait()
    loads[1].wait()
    x = x_ref[...].reshape(pixels, chan_count)
    turned = lax.dot_general(
        x, order_ref[...], OVER_FIRST, preferred_element_type=jnp.float32
    ).astype(jnp.bfloat16)
    flat_ref[...] = jnp.zeros_like(flat_ref)
    flat_ref[:chan_count] = turned
    pl.semaphore_wait(barrier, devices - 1)

    def send_part(part):
        def send(step, carry):
            home = step
            target = device_of(home)
            first = pl.multiple_of(home * chan + offsets[part], SUB)

            @pl.when(target != me)
            def _():
                pltpu.make_async_remote_copy(
                    src_ref=flat_ref.at[pl.ds(first, sizes[part])],
                    dst_ref=arrived_refs[part].at[me],
                    send_sem=block_send_sem,
                    recv_sem=block_recv_sem.at[part],
                    device_id=place(target),
                    device_id_type=MESH,
                ).start()

            return carry

        lax.fori_loop(0, homes, send, 0)

    send_part(0)

    @pl.when(is_home)
    def _():
        for part in range(parts):
            first = pl.multiple_of(own_home * chan + offsets[part], SUB)
            pltpu.make_async_copy(
                flat_ref.at[pl.ds(first, sizes[part])], arrived_refs[part].at[me],
                local_sem.at[part],
            ).start()

    loads[2].wait()
    loads[3].wait()
    lane = lax.broadcasted_iota(jnp.int32, (pixels, 128), 0)
    slot = lax.broadcasted_iota(jnp.int32, (pixels, 128), 1)
    segment = (lane >= slot * cols) & (lane < (slot + 1) * cols)
    segment = jnp.where(segment, 1.0, 0.0).astype(jnp.bfloat16)

    def add_up(cells):
        return jnp.dot(cells, segment, preferred_element_type=jnp.float32)

    cells = flat_ref[...]
    means = add_up(cells) / cols
    near = means.astype(jnp.bfloat16)
    spread_out = lax.dot_general(near, segment, OVER_LAST, preferred_element_type=jnp.float32)
    offset = cells.astype(jnp.float32) - spread_out
    square = offset * offset
    high = square.astype(jnp.bfloat16)
    low = (square - high.astype(jnp.float32)).astype(jnp.bfloat16)
    shift = means - near.astype(jnp.float32)
    squares = jnp.maximum(add_up(high) + add_up(low) - cols * shift * shift, 0.0)
    start, size = group_rows(size_ref, 128, groups)
    member = jnp.where(
        membership(0, homes * chan, start, size)
        & (lax.broadcasted_iota(jnp.int32, (1, 128), 1) < groups),
        1.0, 0.0,
    )
    centre = exact(means, member, OVER_FIRST) / jnp.maximum(size, 1).astype(jnp.float32)
    offset = means - exact(member, centre, OVER_LAST)
    spread = exact(squares + cols * offset * offset, member, OVER_FIRST)
    lanes = report_ref.shape[1]
    rest = lanes - 2 * rows * groups
    place_of = lax.broadcasted_iota(jnp.int32, (1, rest), 1)
    numbers = jnp.zeros((1, rest), jnp.float32)
    for row in range(rows):
        numbers = jnp.where(place_of == row, band_ref[row].astype(jnp.float32), numbers)
    report = jnp.concatenate(
        [centre[row : row + 1, :groups] for row in range(rows)]
        + [spread[row : row + 1, :groups] for row in range(rows)]
        + [numbers],
        axis=1,
    )
    report_ref[...] = report
    reports_ref[me] = report

    def tell(step, carry):
        pltpu.make_async_remote_copy(
            src_ref=report_ref,
            dst_ref=reports_ref.at[me],
            send_sem=report_send_sem,
            recv_sem=report_recv_sem,
            device_id=place(lax.rem(me + step, devices)),
            device_id_type=MESH,
        ).start()
        return carry

    lax.fori_loop(1, devices, tell, 0)
    for part in range(1, parts):
        send_part(part)

    loads[4].wait()
    loads[5].wait()
    wanted = own_home * chan + lax.broadcasted_iota(jnp.int32, (chan, chan_count), 0)
    chosen = jnp.where(
        lax.broadcasted_iota(jnp.int32, (chan, chan_count), 1) == wanted, 1.0, 0.0
    )
    coef = exact(chosen, coef_ref[...], OVER_LAST)
    high = coef.astype(jnp.bfloat16).astype(jnp.float32)
    coef = jnp.concatenate([high, coef - high, high], axis=1).astype(jnp.bfloat16)
    blank = jnp.zeros((basis_ref.shape[1], bins - freq), jnp.float32)

    def generate(n, carry):
        basis = jnp.concatenate(
            [basis_ref[n, :, 0, :], blank, basis_ref[n, :, 1, :], blank], axis=1
        )
        high = basis.astype(jnp.bfloat16).astype(jnp.float32)
        both = jnp.concatenate([high, high, basis - high], axis=0).astype(jnp.bfloat16)
        made = jnp.dot(coef, both, preferred_element_type=jnp.float32)
        kern_ref[n, :chan] = made[:, :bins]
        kern_ref[n, chan:] = made[:, bins:]
        return carry

    lax.fori_loop(0, basis_ref.shape[0], generate, 0, unroll=3)
    for load in loads[6:]:
        load.wait()
    rest = win_ref.shape[1] % 256
    rest = rest if rest <= SUB else 0
    whole = win_ref.shape[1] - rest
    if rest:
        for index, weights in enumerate((win_ref, wout_ref)):
            tail = weights[:, whole:].astype(jnp.float32)
            tail = jnp.concatenate([tail, jnp.zeros((chan_count, 128 - rest), jnp.float32)], axis=1)
            rest_ref[index * SUB : (index + 1) * SUB] = tail.T[:SUB]
    drain(reports_ref, devices - 1, report_send_sem)
    drain(reports_ref, devices - 1, report_recv_sem)

    @pl.when(is_home)
    def _():
        start, size = group_rows(size_ref, lanes, groups)
        amount = size.astype(jnp.float32) * cols
        lane = lax.broadcasted_iota(jnp.int32, (1, lanes), 1)
        seen = []
        for band in range(bands):
            report = reports_ref[band * pieces : (band + 1) * pieces, 0]
            centre = jnp.sum(report, axis=0, keepdims=True) / pieces
            offset = report - centre
            between = amount * jnp.sum(offset * offset, axis=0, keepdims=True)
            within = jnp.sum(report, axis=0, keepdims=True)
            seen.append((report, centre, between, within))
        band_of = []
        for band in range(bands):
            for row in range(rows):
                mark = lane == 2 * rows * groups + row
                number = jnp.sum(jnp.where(mark, seen[band][0][:1], 0.0)).astype(jnp.int32)
                band_of.append(jnp.clip(number, 0, band_count - 1))
        for part in range(parts):
            size_of, arrived_ref, mixed_ref = sizes[part], arrived_refs[part], mixed_refs[part]
            span = lat * size_of
            pltpu.make_async_copy(
                flat_ref.at[pl.ds(0, size_of)], arrived_ref.at[me], local_sem.at[part]
            ).wait()
            drain(arrived_ref, devices - 1, block_recv_sem.at[part])
            member = membership(own_home * chan + offsets[part], size_of, start, size)
            for band in range(bands):
                for piece in range(pieces):
                    cells = arrived_ref[band * pieces + piece].astype(jnp.float32)
                    for row in range(rows):
                        at = (band * rows + row) * size_of
                        wide_ref[at : at + size_of, piece * cols : (piece + 1) * cols] = cells[
                            :, row * cols : (row + 1) * cols
                        ]
            raw = jnp.dot(
                wide_ref[:span].astype(jnp.bfloat16), table_ref[...],
                preferred_element_type=jnp.float32,
            )
            for band in range(bands):
                _, centre, between, within = seen[band]
                for row in range(rows):
                    low, high = row * groups, (rows + row) * groups
                    here = member & (lane >= low) & (lane < low + groups)
                    there = member & (lane >= high) & (lane < high + groups)

                    def pick(mask, cells):
                        return jnp.sum(jnp.where(mask, cells, 0.0), axis=1, keepdims=True)

                    square = pick(here, between) + pick(there, within)
                    count = pick(here, amount) * pieces
                    mean = pick(here, centre)
                    scale = lax.rsqrt(square / jnp.maximum(count, 1.0) + EPSILON)
                    at = (band * rows + row) * size_of
                    spec_ref[at : at + size_of] = (raw[at : at + size_of] - mean * total_ref[...]) * scale
            for row in range(lat):
                real = jnp.zeros((size_of, bins), jnp.float32)
                imag = jnp.zeros((size_of, bins), jnp.float32)
                for tap in range(TAPS):
                    source = row + tap - HALO
                    if source < 0 or source >= lat:
                        continue
                    at = source * size_of
                    spec_real = spec_ref[at : at + size_of, :bins]
                    spec_imag = spec_ref[at : at + size_of, bins:]
                    index = band_of[row] * TAPS + tap
                    at = offsets[part]
                    kern_real = kern_ref[index, at : at + size_of]
                    kern_imag = kern_ref[index, chan + at : chan + at + size_of]
                    real = real + kern_real * spec_real - kern_imag * spec_imag
                    imag = imag + kern_real * spec_imag + kern_imag * spec_real
                prod_ref[row * size_of : (row + 1) * size_of, :bins] = real
                prod_ref[row * size_of : (row + 1) * size_of, bins:] = imag
            corr_ref[:span] = lax.dot_general(
                (prod_ref[:span] * weight_ref[...]).astype(jnp.bfloat16),
                table_ref[...],
                OVER_LAST,
                preferred_element_type=jnp.float32,
            )
            for band in range(bands):
                for piece in range(pieces):
                    pieces_of = []
                    for row in range(rows):
                        at = (band * rows + row) * size_of
                        pieces_of.append(
                            corr_ref[at : at + size_of, piece * cols : (piece + 1) * cols]
                        )
                    device = band * pieces + piece
                    cells = arrived_ref[device].astype(jnp.float32)
                    mixed_ref[device] = (
                        cells + jnp.concatenate(pieces_of, axis=1)
                    ).astype(jnp.bfloat16)
            first = pl.multiple_of(own_home * chan + offsets[part], SUB)

            def give(step, carry):
                target = step

                @pl.when(target != me)
                def _():
                    pltpu.make_async_remote_copy(
                        src_ref=mixed_ref.at[target],
                        dst_ref=returned_ref.at[pl.ds(first, size_of)],
                        send_sem=mixed_send_sem,
                        recv_sem=mixed_recv_sem,
                        device_id=place(target),
                        device_id_type=MESH,
                    ).start()

                return carry

            lax.fori_loop(0, devices, give, 0)
            pltpu.make_async_copy(
                mixed_ref.at[me], returned_ref.at[pl.ds(first, size_of)], local_sem.at[part]
            ).start()
        for part in range(parts):
            pltpu.make_async_copy(
                mixed_refs[part].at[me], returned_ref.at[pl.ds(0, sizes[part])],
                local_sem.at[part],
            ).wait()
            drain(mixed_refs[part], devices - 1, mixed_send_sem)
        drain(flat_ref, (homes - 1) * chan, block_send_sem)
        drain(returned_ref, (homes - 1) * chan, mixed_recv_sem)

    @pl.when(jnp.logical_not(is_home))
    def _():
        drain(flat_ref, homes * chan, block_send_sem)
        drain(returned_ref, homes * chan, mixed_recv_sem)

    def gelu(hidden):
        return (0.5 * hidden * (1.0 + lax.erf(hidden * math.sqrt(0.5)))).astype(jnp.bfloat16)

    step = pixels
    for at in range(0, pixels, step):
        inputs = lax.dot_general(
            order_ref[at : at + step, :], returned_ref[...], OVER_LAST,
            preferred_element_type=jnp.float32,
        )[:, :chan_count]
        centre = jnp.mean(inputs, axis=-1, keepdims=True)
        spread = jnp.mean((inputs - centre) ** 2, axis=-1, keepdims=True)
        normalised = (
            (inputs - centre) * lax.rsqrt(spread + EPSILON) * gain_ref[...].reshape(1, chan_count)
        ).astype(jnp.bfloat16)
        result = inputs
        for unit in range(rest):
            column = rest_ref[unit : unit + 1]
            hidden = jnp.sum(normalised.astype(jnp.float32) * column, axis=1, keepdims=True)
            result = result + gelu(hidden).astype(jnp.float32) * rest_ref[SUB + unit : SUB + unit + 1]
        hidden = jnp.dot(normalised, win_ref[:, :whole], preferred_element_type=jnp.float32)
        result = result + lax.dot_general(
            gelu(hidden), wout_ref[:, :whole], OVER_LAST, preferred_element_type=jnp.float32
        )
        out_ref[at // rows : (at + step) // rows] = result.astype(jnp.bfloat16).reshape(
            step // rows, rows, chan_count
        )


def per_device(fields, group_size, band_of_row, basis_spectra, basis_coef, mlp_gain, w_in, w_out):
    row_count, col_count, chan_count = fields.shape
    pieces = lax.axis_size("lon")
    bands = lax.axis_size("lat")
    devices = pieces * bands
    lon_count = col_count * pieces
    lat_count = row_count * bands
    freq_count = lon_count // 2 + 1
    groups = group_size.shape[0]
    pixels = row_count * col_count
    chan = round_up(-(-chan_count // devices), SUB)
    homes = -(-chan_count // chan)
    sizes = [SUB] + [chan - SUB] * (chan > SUB)
    parts = len(sizes)
    tallest = lat_count * max(sizes)
    bins = round_up(freq_count, 128)
    band_count, _, basis_count = basis_spectra.shape[:3]
    hidden = w_in.shape[1]
    lanes = round_up((2 * groups + 1) * row_count, 128)
    table, total, weight = dft_tables(lon_count, bins)
    basis = basis_spectra.reshape(band_count * TAPS, basis_count, 2, freq_count)
    f32, bf16 = jnp.float32, jnp.bfloat16
    scalars = [group_size, band_of_row]
    operands = [
        (jnp.transpose(fields, (1, 0, 2)), bf16),
        (pixel_order(row_count, col_count), bf16),
        (basis_coef.T, f32),
        (basis, f32),
        (table, bf16),
        (total, f32),
        (weight, f32),
        (mlp_gain, f32),
        (w_in, bf16),
        (w_out.T, bf16),
    ]
    out = pl.pallas_call(
        functools.partial(
            block_body, devices, homes, sizes, freq_count, bins, row_count, col_count,
            chan_count, groups,
        ),
        out_shape=jax.ShapeDtypeStruct((col_count, row_count, chan_count), bf16),
        in_specs=[HBM] * (len(scalars) + len(operands)),
        out_specs=VMEM,
        scratch_shapes=[pltpu.SMEM(array.shape, jnp.int32) for array in scalars]
        + [pltpu.VMEM(array.shape, kind) for array, kind in operands]
        + [
            pltpu.VMEM((homes * chan, pixels), bf16),
            pltpu.VMEM((homes * chan, pixels), bf16),
            pltpu.VMEM((1, lanes), f32),
            pltpu.VMEM((devices, 1, lanes), f32),
            pltpu.VMEM((band_count * TAPS, 2 * chan, bins), f32),
            pltpu.VMEM((tallest, lon_count), f32),
            pltpu.VMEM((tallest, 2 * bins), f32),
            pltpu.VMEM((tallest, 2 * bins), f32),
            pltpu.VMEM((tallest, lon_count), f32),
            pltpu.VMEM((2 * SUB, chan_count), f32),
            DMA((len(scalars) + len(operands),)),
            DMA,
            DMA((parts,)),
            DMA,
            DMA,
            DMA,
            DMA,
            DMA((parts,)),
        ]
        + [pltpu.VMEM((devices, size, pixels), bf16) for size in sizes] * 2,
        compiler_params=pltpu.CompilerParams(
            collective_id=0, has_side_effects=True, vmem_limit_bytes=60 * 1024 * 1024
        ),
    )(*scalars, *[array for array, _ in operands])
    return jnp.transpose(out, (1, 0, 2))


def solution(mesh):
    placed = (P("lat", "lon", None), P(), P("lat"), P(), P(), P(), P(), P())
    return jax.shard_map(
        per_device, mesh=mesh, in_specs=placed, out_specs=P("lat", "lon", None), check_vma=False
    )
```
